512 devices in a mesh: row: 128 (over x, z, core), mp: 4 (over y).
Axes of the slice: x: 4, y: 4, z: 16, core: 2. Of those that a mesh axis runs over, the one named last changes fastest.
Arguments:
- queries: bfloat16 [768, 16384], P('mp', 'row'), may hold values from -36 to 36
- key_cells: bfloat16 [768, 16384], P('mp', 'row'), may hold values from -7 to 7
- value_cells: bfloat16 [768, 16384], P('mp', 'row'), may hold values from -6 to 6
- out_weight: bfloat16 [768, 768], P('mp'), may hold values from -0.21875 to 0.21875
- out_cotangent: bfloat16 [768, 16384], P('mp', 'row'), may hold values from -6 to 6
- parent_rows: int32 [128, 64], P('row'), may hold values from 0 to 1023, as said below
- window_reach: int32 [128], P('row'), may hold values from 0 to 1
- valid_cells: int32 [128], P('row'), may hold values from 64 to 128, as said below
Outputs:
- mixed: bfloat16 [768, 16384], P('mp', 'row')
- d_queries: bfloat16 [768, 16384], P('mp', 'row')
- d_key_cells: bfloat16 [768, 16384], P('mp', 'row')
- d_value_cells: bfloat16 [768, 16384], P('mp', 'row')
- weight_grad: float32 [768, 768], P('mp')
The draws below stay inside these ranges and needn't reach their ends.
Inputs may be any that keep to these rules, and one draw needn't show every extreme that they name: `parent_rows`: the rows named by the blocks of one device (the 1 block in a row of the array that share an index of row) lie on pairwise different devices, where a device holds 8 consecutive rows; every named row lies wholly below its block's valid_cells. `valid_cells`: A multiple of 16.
All inputs are finite; a program needn't handle non-finite values.
Results may differ from the reference program's by a relative error of at most 0.012.
Values may be sent and summed in bfloat16 or wider, within the bound.
A program may use at most 64 MiB of HBM per device.

```python
import jax
import jax.numpy as jnp
from jax import lax

D = 768
HEADS = 12
HEAD_DIM = 64
CELLS_BLK = 128
ROW_CELLS = 16
ROWS_BLK = 8
BLK_DEV = 1
FANOUT = 64
NBLK = 128
CELLS = 16384
N_ROW = 128


def normal_field(key, salt):
    return jnp.clip(jax.random.normal(jax.random.fold_in(key, salt), (CELLS, D), jnp.float32), -6.0, 6.0)


def draw_key_cells(key, part):
    field = normal_field(key, 11)
    return field.T.astype(jnp.bfloat16)


def draw_queries(key, part):
    field = normal_field(key, 15)
    return field.T.astype(jnp.bfloat16)


def valid_rows(key):
    counts = jax.random.randint(jax.random.fold_in(key, 21), (NBLK,), ROWS_BLK // 2, ROWS_BLK + 1)
    full_block = jax.random.randint(jax.random.fold_in(key, 22), (), 0, NBLK)
    return jnp.where(jnp.arange(NBLK) == full_block, ROWS_BLK, counts).astype(jnp.int32)


def draw_valid_cells(key, part):
    return (valid_rows(key) * ROW_CELLS).astype(jnp.int32)


def draw_parent_rows(key, part):
    counts = valid_rows(key)
    wanted = BLK_DEV * FANOUT
    hot_count = max(1, N_ROW // 8)
    hot_owner = (jax.random.permutation(jax.random.fold_in(key, 31), N_ROW) < hot_count).astype(jnp.int32)
    noise = jax.random.randint(jax.random.fold_in(key, 32), (N_ROW, N_ROW), 0, 4096)
    ranking = (noise + 8192 * hot_owner[None, :]) * N_ROW + jnp.arange(N_ROW)[None, :]
    owners = lax.top_k(ranking, wanted)[1]
    owners = jax.random.permutation(jax.random.fold_in(key, 33), owners, axis=1, independent=True)
    local_block = jax.random.randint(jax.random.fold_in(key, 34), (N_ROW, wanted), 0, BLK_DEV)
    blocks = owners * BLK_DEV + local_block
    offsets = jax.random.randint(jax.random.fold_in(key, 35), (N_ROW, wanted), 0, 1 << 16)
    within = offsets % counts[blocks]
    return (blocks * ROWS_BLK + within).reshape(NBLK, FANOUT).astype(jnp.int32)


def place_ends(array, rng, smallest, top_value):
    longest = array.shape.index(max(array.shape))
    spots = []
    for shift in (0, 1):
        where = [jax.random.randint(jax.random.fold_in(rng, axis), (), 0, length) for axis, length in enumerate(array.shape)]
        where[longest] = (where[longest] + shift) % array.shape[longest]
        spots.append(tuple(where))
    return array.at[spots[0]].set(smallest).at[spots[1]].set(top_value)


def block_scale(rng, shape, pieces, low, top_value):
    level, own = 1.0, jax.random.fold_in(rng, 6)
    for axis_at, blocks in pieces:
        draws = jnp.exp(jax.random.uniform(jax.random.fold_in(own, axis_at), (blocks,), jnp.float32, low / len(pieces), top_value / len(pieces)))
        level = level * jnp.repeat(draws, shape[axis_at] // blocks).reshape([-1 if axis == axis_at else 1 for axis in range(len(shape))])
    return level


def normal_values(own_key, shape, width, bound, cuts=(), kind=jnp.bfloat16):
    level = block_scale(own_key, shape, cuts, -0.22, 0.18) if cuts else 1.0
    drawn = jax.random.normal(own_key, shape, jnp.float32) * width * level
    return jnp.minimum(jnp.maximum(drawn, -bound), bound).astype(kind)


def setup_inputs(seed: int = 0) -> dict:
    arg_keys = jax.random.split(jax.random.key(seed), 9)
    return {
        "queries": draw_queries(jax.random.fold_in(arg_keys[8], 71), 0),
        "key_cells": draw_key_cells(jax.random.fold_in(arg_keys[8], 71), 0),
        "value_cells": normal_values(arg_keys[2], (D, CELLS), 1.0, 6.0, ((0, 4), (1, 128))),
        "out_weight": normal_values(arg_keys[3], (D, D), D ** -0.5, 0.21875, ((0, 4),)),
        "out_cotangent": normal_values(arg_keys[4], (D, CELLS), 1.0, 6.0, ((0, 4), (1, 128))),
        "parent_rows": draw_parent_rows(jax.random.fold_in(arg_keys[8], 71), 0),
        "window_reach": place_ends(jax.random.randint(arg_keys[6], (NBLK,), 0, 2), jax.random.fold_in(arg_keys[6], 1), 0, 1).astype(jnp.int32),
        "valid_cells": draw_valid_cells(jax.random.fold_in(arg_keys[8], 71), 0),
    }


def masked_softmax(scores, visible):
    masked = jnp.where(visible, scores, -1e30)
    top_score = jnp.max(masked, axis=-1, keepdims=True)
    exponent = jnp.exp(jnp.where(visible, scores - top_score, -1e30))
    return exponent / jnp.sum(exponent, axis=-1, keepdims=True)


def reference(queries, key_cells, value_cells, out_weight, out_cotangent, parent_rows, window_reach, valid_cells):
    queries = queries.T
    key_cells = key_cells.T
    value_cells = value_cells.T
    out_cotangent = out_cotangent.T
    block_count = valid_cells.shape[0]
    feature_width = queries.shape[1]
    score_scale = HEAD_DIM ** -0.5
    query_blocks = queries.reshape(block_count, CELLS_BLK, feature_width)
    key_blocks = key_cells.reshape(block_count, CELLS_BLK, feature_width)
    value_blocks = value_cells.reshape(block_count, CELLS_BLK, feature_width)
    zero_block = jnp.zeros((1, CELLS_BLK, feature_width), key_cells.dtype)
    prior_keys = jnp.concatenate([zero_block, key_blocks[:-1]], axis=0)
    prior_values = jnp.concatenate([zero_block, value_blocks[:-1]], axis=0)
    key_table = key_cells.reshape(block_count * ROWS_BLK, ROW_CELLS, feature_width)
    value_table = value_cells.reshape(block_count * ROWS_BLK, ROW_CELLS, feature_width)
    cell_ids = jnp.arange(CELLS_BLK)
    own_ok = cell_ids[None, :] < valid_cells[:, None]
    prior_valid = jnp.concatenate([jnp.zeros((1, CELLS_BLK), bool), own_ok[:-1]], axis=0)
    prior_ok = prior_valid & (window_reach[:, None] == 1)
    parent_ok = jnp.ones((block_count, FANOUT * ROW_CELLS), bool)
    key_mask = jnp.concatenate([prior_ok, own_ok, parent_ok], axis=1)

    def block_keys(index):
        named = parent_rows[index]
        parent_keys = key_table[named].reshape(FANOUT * ROW_CELLS, feature_width)
        parent_values = value_table[named].reshape(FANOUT * ROW_CELLS, feature_width)
        all_keys = jnp.concatenate([prior_keys[index], key_blocks[index], parent_keys], axis=0)
        all_values = jnp.concatenate([prior_values[index], value_blocks[index], parent_values], axis=0)
        return all_keys, all_values

    def block_probs(index, all_keys):
        query_heads = query_blocks[index].astype(jnp.float32).reshape(CELLS_BLK, HEADS, HEAD_DIM)
        key_heads = all_keys.astype(jnp.float32).reshape(-1, HEADS, HEAD_DIM)
        scores = jnp.einsum('qhd,khd->hqk', query_heads, key_heads) * score_scale
        return masked_softmax(scores, key_mask[index][None, None, :])

    def forward_block(index):
        all_keys, all_values = block_keys(index)
        probs = block_probs(index, all_keys)
        probs_low = lax.optimization_barrier(probs.astype(jnp.bfloat16)).astype(jnp.float32)
        value_heads = all_values.astype(jnp.float32).reshape(-1, HEADS, HEAD_DIM)
        attended = jnp.einsum('hqk,khd->qhd', probs_low, value_heads)
        return attended.reshape(CELLS_BLK, feature_width).astype(jnp.bfloat16)

    attended = lax.map(forward_block, jnp.arange(block_count)).reshape(-1, feature_width)
    mixed = jnp.dot(attended, out_weight, preferred_element_type=jnp.float32).astype(jnp.bfloat16)
    d_attended = lax.dot_general(out_cotangent, out_weight, (((1,), (1,)), ((), ())), preferred_element_type=jnp.float32).astype(jnp.bfloat16)
    weight_grad = lax.dot_general(attended, out_cotangent, (((0,), (0,)), ((), ())), preferred_element_type=jnp.float32)
    d_blocks = d_attended.reshape(block_count, CELLS_BLK, feature_width)

    def backward_block(carry, index):
        key_total, value_total = carry
        all_keys, all_values = block_keys(index)
        probs = block_probs(index, all_keys)
        probs_low = lax.optimization_barrier(probs.astype(jnp.bfloat16)).astype(jnp.float32)
        d_heads = d_blocks[index].astype(jnp.float32).reshape(CELLS_BLK, HEADS, HEAD_DIM)
        value_heads = all_values.astype(jnp.float32).reshape(-1, HEADS, HEAD_DIM)
        key_heads = all_keys.astype(jnp.float32).reshape(-1, HEADS, HEAD_DIM)
        query_heads = query_blocks[index].astype(jnp.float32).reshape(CELLS_BLK, HEADS, HEAD_DIM)
        d_probs = jnp.einsum('qhd,khd->hqk', d_heads, value_heads)
        row_delta = jnp.sum(probs * d_probs, axis=-1, keepdims=True)
        d_scores = probs * (d_probs - row_delta) * score_scale
        d_scores = lax.optimization_barrier(d_scores.astype(jnp.bfloat16)).astype(jnp.float32)
        d_query = jnp.einsum('hqk,khd->qhd', d_scores, key_heads).reshape(CELLS_BLK, feature_width).astype(jnp.bfloat16)
        d_keys = jnp.einsum('hqk,qhd->khd', d_scores, query_heads).reshape(-1, feature_width)
        d_values = jnp.einsum('hqk,qhd->khd', probs_low, d_heads).reshape(-1, feature_width)
        earlier = jnp.maximum(index - 1, 0)
        key_total = key_total.at[earlier].add(d_keys[:CELLS_BLK])
        value_total = value_total.at[earlier].add(d_values[:CELLS_BLK])
        key_total = key_total.at[index].add(d_keys[CELLS_BLK:2 * CELLS_BLK])
        value_total = value_total.at[index].add(d_values[CELLS_BLK:2 * CELLS_BLK])
        named = parent_rows[index]
        key_total = key_total.reshape(-1, ROW_CELLS, feature_width).at[named].add(
            d_keys[2 * CELLS_BLK:].reshape(FANOUT, ROW_CELLS, feature_width)).reshape(block_count, CELLS_BLK, feature_width)
        value_total = value_total.reshape(-1, ROW_CELLS, feature_width).at[named].add(
            d_values[2 * CELLS_BLK:].reshape(FANOUT, ROW_CELLS, feature_width)).reshape(block_count, CELLS_BLK, feature_width)
        return (key_total, value_total), d_query

    zero_total = jnp.zeros((block_count, CELLS_BLK, feature_width), jnp.float32)
    totals, d_queries = lax.scan(backward_block, (zero_total, zero_total), jnp.arange(block_count))
    d_queries = d_queries.reshape(-1, feature_width)
    d_key_cells = totals[0].reshape(-1, feature_width).astype(jnp.bfloat16)
    d_value_cells = totals[1].reshape(-1, feature_width).astype(jnp.bfloat16)
    return (mixed.T, d_queries.T, d_key_cells.T, d_value_cells.T, weight_grad)
```

```python
import jax
import jax.numpy as jnp
from jax import lax
from jax.experimental import pallas as pl
from jax.experimental.pallas import tpu as pltpu
from jax.sharding import Mesh, PartitionSpec as P

HEAD_DIM = 64
CELLS_BLK = 128
ROW_CELLS = 16
ROWS_BLK = 8
NX, NZ, NC = 4, 16, 2
ROW = ("x", "z", "c")
SIDE = ("x", "c")
NSIDE = NX * NC
SLOTS = NSIDE * NZ
KEYS = 2 * CELLS_BLK + SLOTS * ROW_CELLS


def shifted(block, distance):
    devices = range(NX * NZ * NC)
    route = [(i - distance, i) for i in devices if i - distance in devices]
    return lax.ppermute(block, ROW, route)


def attend_kernel(
    q_ref, da_ref, prior_ref, own_ref, slots_ref, seen_ref, att_ref, dq_ref, dprior_ref, down_ref, dslots_ref
):
    scale = HEAD_DIM ** (-0.5)
    kv = jnp.concatenate([prior_ref[...], own_ref[...], slots_ref[...]], axis=0)
    q, da = q_ref[...], da_ref[...]
    blank = jnp.zeros_like(q)
    both = jnp.concatenate(
        [jnp.concatenate([q, blank], axis=1), jnp.concatenate([blank, da], axis=1)], axis=0
    )
    cross = jnp.dot(kv, both, preferred_element_type=jnp.float32)
    visible = seen_ref[...] > 0.5
    scores = jnp.where(visible, cross[:, :CELLS_BLK] * scale, -1e30)
    top = jnp.max(scores, axis=0, keepdims=True)
    grown = jnp.where(visible, jnp.exp(scores - top), 0.0)
    probs = grown / jnp.sum(grown, axis=0, keepdims=True)
    probs_low = probs.astype(jnp.bfloat16)
    d_probs = cross[:, CELLS_BLK:]
    delta = jnp.sum(probs * d_probs, axis=0, keepdims=True)
    d_scores = (probs * (d_probs - delta) * scale).astype(jnp.bfloat16)
    pair = jnp.concatenate([d_scores, probs_low], axis=1)
    d_kv = lax.dot_general(pair, both, (((1,), (1,)), ((), ())), preferred_element_type=jnp.float32)
    mixed = lax.dot_general(kv, pair, (((0,), (0,)), ((), ())), preferred_element_type=jnp.float32)
    dq_ref[...] = mixed[:HEAD_DIM, :CELLS_BLK].astype(jnp.bfloat16)
    att_ref[...] = mixed[HEAD_DIM:, CELLS_BLK:].astype(jnp.bfloat16)
    dprior_ref[...] = d_kv[:CELLS_BLK].astype(jnp.bfloat16)
    down_ref[...] = d_kv[CELLS_BLK : 2 * CELLS_BLK]
    dslots_ref[...] = d_kv[2 * CELLS_BLK :].astype(jnp.bfloat16)


def attend(q, da, prior, own, slots, seen):
    heads = q.shape[0] // HEAD_DIM
    width = own.shape[1]
    feat = pl.BlockSpec((HEAD_DIM, CELLS_BLK), lambda h: (h, 0))
    cells = pl.BlockSpec((CELLS_BLK, 2 * HEAD_DIM), lambda h: (0, h))
    many = pl.BlockSpec((SLOTS * ROW_CELLS, 2 * HEAD_DIM), lambda h: (0, h))
    bf, f32 = jnp.bfloat16, jnp.float32
    return pl.pallas_call(
        attend_kernel,
        grid=(heads,),
        in_specs=[feat, feat, cells, cells, many, pl.BlockSpec((KEYS, 1), lambda h: (0, 0))],
        out_specs=[feat, feat, cells, cells, many],
        out_shape=[
            jax.ShapeDtypeStruct(q.shape, bf),
            jax.ShapeDtypeStruct(q.shape, bf),
            jax.ShapeDtypeStruct((CELLS_BLK, width), bf),
            jax.ShapeDtypeStruct((CELLS_BLK, width), f32),
            jax.ShapeDtypeStruct((SLOTS * ROW_CELLS, width), bf),
        ],
        name="attend",
    )(q, da, prior, own, slots, seen)


def pick_kernel(index_ref, table_ref, out_ref):
    for peer in range(NSIDE):
        for z in range(NZ):
            out_ref[peer, z] = table_ref[z, index_ref[peer, z]]


def pick(index, table):
    return pl.pallas_call(
        pick_kernel,
        in_specs=[pl.BlockSpec(memory_space=pltpu.SMEM), pl.BlockSpec(memory_space=pltpu.VMEM)],
        out_specs=pl.BlockSpec(memory_space=pltpu.VMEM),
        out_shape=jax.ShapeDtypeStruct((NSIDE, NZ) + table.shape[2:], table.dtype),
        name="pick",
    )(index, table)


def gather_back_kernel(index_ref, parts_ref, out_ref, total):
    for z in range(NZ):
        total[...] = jnp.zeros_like(total)
        for peer in range(NSIDE):
            spot = index_ref[peer, z]
            total[spot] = total[spot] + parts_ref[peer, z].astype(jnp.float32)
        out_ref[z] = total[...].astype(out_ref.dtype)


def gather_back(index, parts):
    tail = parts.shape[2:]
    return pl.pallas_call(
        gather_back_kernel,
        in_specs=[pl.BlockSpec(memory_space=pltpu.SMEM), pl.BlockSpec(memory_space=pltpu.VMEM)],
        out_specs=pl.BlockSpec(memory_space=pltpu.VMEM),
        out_shape=jax.ShapeDtypeStruct((NZ, ROWS_BLK) + tail, parts.dtype),
        scratch_shapes=[pltpu.VMEM((ROWS_BLK,) + tail, jnp.float32)],
        name="gather_back",
    )(index, parts)


def on_device(
    queries, key_cells, value_cells, out_weight, out_cotangent, parent_rows, window_reach, valid_cells
):
    bf, f32 = jnp.bfloat16, jnp.float32
    features = queries.shape[0]
    heads = features // HEAD_DIM
    width = 2 * features
    x_at, z_at, c_at = (lax.axis_index(name) for name in ROW)
    block_id = (x_at * NZ + z_at) * NC + c_at
    valid = valid_cells[0]
    pairs = jnp.concatenate(
        [key_cells.reshape(heads, HEAD_DIM, -1), value_cells.reshape(heads, HEAD_DIM, -1)], axis=1
    )
    own = pairs.reshape(width, CELLS_BLK).T
    table = lax.all_gather(own.reshape(ROWS_BLK, ROW_CELLS, width), "z")
    told = jnp.full((ROW_CELLS, width), valid.astype(bf))
    from_prior = shifted(jnp.concatenate([own, told], axis=0), 1)
    prior = from_prior[:CELLS_BLK]
    prior_valid = from_prior[CELLS_BLK, 0].astype(jnp.int32)

    wanted = parent_rows.reshape(-1)
    asked = lax.all_gather(wanted, SIDE)
    owner_here = (x_at * NZ + jnp.arange(NZ)) * NC + c_at
    hit = (asked // ROWS_BLK)[:, None, :] == owner_here[None, :, None]
    index = jnp.sum(jnp.where(hit, (asked % ROWS_BLK)[:, None, :], 0), axis=-1)
    side_ids = jnp.arange(NSIDE)
    slot_owner = ((side_ids // NC)[:, None] * NZ + jnp.arange(NZ)[None, :]) * NC + (side_ids % NC)[:, None]
    slot_seen = jnp.any(slot_owner.reshape(-1)[:, None] == (wanted // ROWS_BLK)[None, :], axis=-1)
    cell_ids = jnp.arange(CELLS_BLK)
    prior_seen = (cell_ids < prior_valid) & (window_reach[0] == 1) & (block_id > 0)
    seen = jnp.concatenate([prior_seen, cell_ids < valid, jnp.repeat(slot_seen, ROW_CELLS)])
    seen = seen.astype(f32)[:, None]

    slots = lax.all_to_all(pick(index, table), SIDE, split_axis=0, concat_axis=0, tiled=True)
    cotangent_all = lax.all_gather(out_cotangent, "mp", axis=0, tiled=True)
    d_attended = jnp.dot(out_weight, cotangent_all, preferred_element_type=f32).astype(bf)
    attended, d_queries, d_prior, d_own, d_slots = attend(
        queries, d_attended, prior, own, slots.reshape(SLOTS * ROW_CELLS, width), seen
    )
    parts = lax.all_to_all(
        d_slots.reshape(NSIDE, NZ, ROW_CELLS, width), SIDE, split_axis=0, concat_axis=0, tiled=True
    )
    returned = shifted(d_prior, -1)
    weight_part = lax.dot_general(
        attended, cotangent_all, (((1,), (1,)), ((), ())), preferred_element_type=f32
    )
    depth = features // NSIDE
    weight_split = lax.all_to_all(
        weight_part.astype(bf).reshape(NSIDE, depth, -1), SIDE, split_axis=0, concat_axis=0, tiled=True
    )
    weight_mine = lax.psum(jnp.sum(weight_split.astype(f32), axis=0), "z")
    weight_grad = lax.all_gather(weight_mine, SIDE, axis=0, tiled=True)
    partial_out = lax.dot_general(
        out_weight, attended, (((0,), (0,)), ((), ())), preferred_element_type=f32
    )
    mixed = lax.psum_scatter(partial_out.astype(bf), "mp", scatter_dimension=0, tiled=True)
    owner_parts = lax.psum_scatter(gather_back(index, parts), "z", scatter_dimension=0, tiled=False)
    total = d_own + returned.astype(f32) + owner_parts.reshape(CELLS_BLK, width).astype(f32)
    d_pairs = total.astype(bf).T.reshape(heads, 2, HEAD_DIM, CELLS_BLK)
    d_key_cells = d_pairs[:, 0].reshape(features, CELLS_BLK)
    d_value_cells = d_pairs[:, 1].reshape(features, CELLS_BLK)
    return mixed, d_queries, d_key_cells, d_value_cells, weight_grad


def solution(mesh):
    fine = Mesh(mesh.devices.reshape(NX, NZ, NC, -1), ROW + ("mp",))
    split = P("mp", ROW)
    return jax.shard_map(
        on_device,
        mesh=fine,
        in_specs=(split, split, split, P("mp", None), split, P(ROW, None), P(ROW), P(ROW)),
        out_specs=(split, split, split, split, P("mp", None)),
        check_vma=False,
    )
```

```python
import functools

import jax
import jax.numpy as jnp
from jax import lax
from jax.experimental import pallas as pl
from jax.experimental.pallas import tpu as pltpu
from jax.sharding import Mesh, PartitionSpec as P

HEAD_DIM = 64
CELLS_BLK = 128
ROW_CELLS = 16
ROWS_BLK = 8
NX, NZ, NC = 4, 16, 2
ROW = ("x", "z", "c")
NSIDE = NX * NC
SLOTS = NSIDE * NZ
KEYS = 2 * CELLS_BLK + SLOTS * ROW_CELLS


def attend_kernel(
    q_ref, da_ref, prior_ref, own_ref, slots_ref, seen_ref, att_ref, dq_ref, dprior_ref, down_ref, dslots_ref
):
    scale = HEAD_DIM ** (-0.5)
    kv = jnp.concatenate([prior_ref[...], own_ref[...], slots_ref[...]], axis=0)
    q, da = q_ref[...], da_ref[...]
    blank = jnp.zeros_like(q)
    both = jnp.concatenate(
        [jnp.concatenate([q, blank], axis=1), jnp.concatenate([blank, da], axis=1)], axis=0
    )
    cross = jnp.dot(kv, both, preferred_element_type=jnp.float32)
    visible = seen_ref[...] > 0.5
    scores = jnp.where(visible, cross[:, :CELLS_BLK] * scale, -1e30)
    top = jnp.max(scores, axis=0, keepdims=True)
    grown = jnp.where(visible, jnp.exp(scores - top), 0.0)
    probs = grown / jnp.sum(grown, axis=0, keepdims=True)
    probs_low = probs.astype(jnp.bfloat16)
    d_probs = cross[:, CELLS_BLK:]
    delta = jnp.sum(probs * d_probs, axis=0, keepdims=True)
    d_scores = (probs * (d_probs - delta) * scale).astype(jnp.bfloat16)
    pair = jnp.concatenate([d_scores, probs_low], axis=1)
    d_kv = lax.dot_general(pair, both, (((1,), (1,)), ((), ())), preferred_element_type=jnp.float32)
    mixed = lax.dot_general(kv, pair, (((0,), (0,)), ((), ())), preferred_element_type=jnp.float32)
    dq_ref[...] = mixed[:HEAD_DIM, :CELLS_BLK].astype(jnp.bfloat16)
    att_ref[...] = mixed[HEAD_DIM:, CELLS_BLK:].astype(jnp.bfloat16)
    dprior_ref[...] = d_kv[:CELLS_BLK].astype(jnp.bfloat16)
    down_ref[...] = d_kv[CELLS_BLK : 2 * CELLS_BLK]
    dslots_ref[...] = d_kv[2 * CELLS_BLK :].astype(jnp.bfloat16)


def attend(q, da, prior, own, slots, seen):
    heads = q.shape[0] // HEAD_DIM
    width = own.shape[1]
    feat = pl.BlockSpec((HEAD_DIM, CELLS_BLK), lambda h: (h, 0))
    cells = pl.BlockSpec((CELLS_BLK, 2 * HEAD_DIM), lambda h: (0, h))
    many = pl.BlockSpec((SLOTS * ROW_CELLS, 2 * HEAD_DIM), lambda h: (0, h))
    bf, f32 = jnp.bfloat16, jnp.float32
    return pl.pallas_call(
        attend_kernel,
        grid=(heads,),
        in_specs=[feat, feat, cells, cells, many, pl.BlockSpec((KEYS, 1), lambda h: (0, 0))],
        out_specs=[feat, feat, cells, cells, many],
        out_shape=[
            jax.ShapeDtypeStruct(q.shape, bf),
            jax.ShapeDtypeStruct(q.shape, bf),
            jax.ShapeDtypeStruct((CELLS_BLK, width), bf),
            jax.ShapeDtypeStruct((CELLS_BLK, width), f32),
            jax.ShapeDtypeStruct((SLOTS * ROW_CELLS, width), bf),
        ],
        name="attend",
    )(q, da, prior, own, slots, seen)


MESH = pl.DeviceIdType.MESH
HOPS = (NZ // 2, NZ - NZ // 2 - 1)
HALF = ROWS_BLK // 2
SPARE = 16


def remote(source, target, sems, spot, device):
    return pltpu.make_async_remote_copy(
        src_ref=source,
        dst_ref=target,
        send_sem=sems[0].at[spot],
        recv_sem=sems[1].at[spot],
        device_id=device,
        device_id_type=MESH,
    )


def step_round(place, distance, size):
    return lax.rem(place + (distance % size), size)


def side_device(side):
    return {"x": lax.div(side, NC), "c": lax.rem(side, NC)}


def line_device(x, z, c, distance):
    line = step_round((x * NZ + z) * NC + c, distance, NX * NZ * NC)
    return {"x": lax.div(line, NZ * NC), "z": lax.rem(lax.div(line, NC), NZ), "c": lax.rem(line, NC)}


def meet(peers):
    barrier = pltpu.get_barrier_semaphore()
    for peer in peers:
        pl.semaphore_signal(barrier, inc=1, device_id=peer, device_id_type=MESH)
    pl.semaphore_wait(barrier, len(peers))


def side_peers(side):
    return [side_device(step_round(side, d, NSIDE)) for d in range(1, NSIDE)]


def fetch_kernel(
    nmp, own_ref, info_ref, cot_ref, table_ref, asked_ref, cots_ref, prior_ref, told_ref,
    ring_send, ring_recv, side_send, side_recv, mp_send, mp_recv, line_send, line_recv,
):
    x, z, c, mp = (lax.axis_index(name) for name in ROW + ("mp",))
    side = x * NC + c
    ways = [{"z": step_round(z, 1, NZ)}, {"z": step_round(z, -1, NZ)}]
    after, before = line_device(x, z, c, 1), line_device(x, z, c, -1)
    mp_peers = [{"mp": step_round(mp, d, nmp)} for d in range(1, nmp)]
    meet(ways + side_peers(side) + mp_peers + [after, before])
    ring = {}

    def hop(way, s, half):
        rows = pl.ds(half * HALF, HALF)
        block = step_round(z, s if way else -s, NZ)
        source = table_ref.at[block, rows] if s else own_ref.at[rows]
        copy = remote(source, table_ref.at[block, rows], (ring_send, ring_recv), (way, s, half), ways[way])
        copy.start()
        ring[way, s, half] = copy

    for half in range(2):
        for way in range(2):
            hop(way, 0, half)
    others = []
    for d, peer in enumerate(side_peers(side)):
        others.append(remote(info_ref, asked_ref.at[side], (side_send, side_recv), d, peer))
    for d, peer in enumerate(mp_peers):
        others.append(remote(cot_ref, cots_ref.at[mp], (mp_send, mp_recv), d, peer))
    others.append(remote(own_ref, prior_ref, (line_send, line_recv), 0, after))
    others.append(remote(info_ref, told_ref, (line_send, line_recv), 1, after))
    for copy in others:
        copy.start()
    table_ref[z] = own_ref[...]
    asked_ref[side] = info_ref[...]
    cots_ref[mp] = cot_ref[...]
    for s in range(1, HOPS[0]):
        for half in range(2):
            for way in range(2):
                if s < HOPS[way]:
                    ring[way, s - 1, half].wait_recv()
                    hop(way, s, half)
    for half in range(2):
        for way in range(2):
            ring[way, HOPS[way] - 1, half].wait_recv()
    for copy in others:
        copy.wait()
    for copy in ring.values():
        copy.wait_send()


def vmem():
    return pl.BlockSpec(memory_space=pltpu.VMEM)


def pair_sems(*shape):
    return [pltpu.SemaphoreType.DMA(shape), pltpu.SemaphoreType.DMA(shape)]


def fetch(own, info, cot, nmp):
    bf, i32 = jnp.bfloat16, jnp.int32
    shapes = [
        ((NZ,) + own.shape, bf),
        ((NSIDE,) + info.shape, i32),
        ((nmp,) + cot.shape, bf),
        (own.shape, bf),
        (info.shape, i32),
    ]
    return pl.pallas_call(
        functools.partial(fetch_kernel, nmp),
        in_specs=[vmem()] * 3,
        out_specs=[vmem()] * 5,
        out_shape=[jax.ShapeDtypeStruct(*shape) for shape in shapes],
        scratch_shapes=pair_sems(2, HOPS[0], 2) + pair_sems(NSIDE - 1) + pair_sems(nmp - 1) + pair_sems(2),
        compiler_params=pltpu.CompilerParams(collective_id=0, has_side_effects=True),
        name="fetch",
    )(own, info, cot)


def spread_kernel(index_ref, table_ref, slots_ref, held, side_send, side_recv):
    side = lax.axis_index("x") * NC + lax.axis_index("c")
    peers = side_peers(side)
    meet(peers)
    copies = []
    for d in FAR_FIRST:
        to = step_round(side, d + 1, NSIDE)
        for z in range(NZ):
            held[d, z] = table_ref[z, index_ref[to, z]]
        copy = remote(held.at[d], slots_ref.at[side], (side_send, side_recv), d, peers[d])
        copy.start()
        copies.append(copy)
    for z in range(NZ):
        slots_ref[side, z] = table_ref[z, index_ref[side, z]]
    for copy in copies:
        copy.wait()


FAR_FIRST = (3, 2, 4, 1, 5, 0, 6)


def spread(index, table):
    tail = table.shape[2:]
    return pl.pallas_call(
        spread_kernel,
        in_specs=[pl.BlockSpec(memory_space=pltpu.SMEM), vmem()],
        out_specs=vmem(),
        out_shape=jax.ShapeDtypeStruct((NSIDE, NZ) + tail, table.dtype),
        scratch_shapes=[pltpu.VMEM((NSIDE - 1, NZ) + tail, table.dtype)] + pair_sems(NSIDE - 1),
        compiler_params=pltpu.CompilerParams(collective_id=1, has_side_effects=True),
        name="spread",
    )(index, table)


def settle_kernel(
    nmp, index_ref, slots_ref, dprior_ref, down_ref, out_ref, weight_ref, total_ref, mixed_ref, wall_ref,
    parts, share, sent, got, back, mixes, wside, wsum, wz, wone, wring,
    ring_send, ring_recv, side_send, side_recv, mp_send, mp_recv, line_send, line_recv,
    w1_send, w1_recv, w2_send, w2_recv, w3_send, w3_recv, w4_send, w4_recv,
):
    bf, f32 = jnp.bfloat16, jnp.float32
    x, z, c, mp = (lax.axis_index(name) for name in ROW + ("mp",))
    side = x * NC + c
    z_peers = [{"z": step_round(z, d, NZ)} for d in range(1, NZ)]
    ways = [z_peers[0], z_peers[-1]]
    after, before = line_device(x, z, c, 1), line_device(x, z, c, -1)
    mp_peers = [{"mp": step_round(mp, d, nmp)} for d in range(1, nmp)]
    peers = side_peers(side)
    meet(z_peers + peers + mp_peers + [after, before])
    side_copies, w1, others = [], [], []
    for d in FAR_FIRST:
        to = step_round(side, d + 1, NSIDE)
        side_copies.append(remote(slots_ref.at[to], parts.at[side], (side_send, side_recv), d, peers[d]))
        w1.append(remote(weight_ref.at[to], wside.at[side], (w1_send, w1_recv), d, peers[d]))
    for d, peer in enumerate(mp_peers):
        to = step_round(mp, d + 1, nmp)
        others.append(remote(out_ref.at[to], mixes.at[mp], (mp_send, mp_recv), d, peer))
    others.append(remote(dprior_ref, back, (line_send, line_recv), 0, before))
    for copy in side_copies + w1 + others:
        copy.start()
    parts[side] = slots_ref[side]
    wside[side] = weight_ref[side]
    mixes[mp] = out_ref[mp]
    for copy in side_copies:
        copy.wait_recv()

    def fill(t, carry):
        for row in range(ROWS_BLK):
            total = jnp.zeros(parts.shape[2:], f32)
            for peer in range(NSIDE):
                mark = jnp.where(index_ref[peer, t] == row, 1.0, 0.0)
                total = total + parts[peer, t].astype(f32) * mark
            share[t, row] = total
        return carry

    lax.fori_loop(0, NZ, fill, 0)
    ring = {}
    w2, w3, w4 = [], [], []
    for s in range(HOPS[0]):
        for half in range(2):
            rows = pl.ds(half * HALF, HALF)
            for way in range(2):
                if s >= HOPS[way]:
                    continue
                target = step_round(z, s - HOPS[1] if way else HOPS[0] - s, NZ)
                mine = share[target, rows]
                if s:
                    ring[way, s - 1, half].wait_recv()
                    mine = mine + got[way, s - 1, rows].astype(f32)
                sent[way, s, rows] = mine.astype(bf)
                copy = remote(
                    sent.at[way, s, rows], got.at[way, s, rows], (ring_send, ring_recv), (way, s, half), ways[way]
                )
                copy.start()
                ring[way, s, half] = copy
        if s == 0:
            for copy in w1:
                copy.wait_recv()
            summed = wside[0].astype(f32)
            for peer in range(1, NSIDE):
                summed = summed + wside[peer].astype(f32)
            wsum[...] = summed.astype(bf)
            for d, peer in enumerate(z_peers):
                to = step_round(z, d + 1, NZ)
                w2.append(remote(wsum.at[to], wz.at[z], (w2_send, w2_recv), d, peer))
                w2[-1].start()
            wz[z] = wsum[z]
        if s == 3:
            for copy in w2:
                copy.wait_recv()
            one = wz[0].astype(f32)
            for peer in range(1, NZ):
                one = one + wz[peer].astype(f32)
            wone[...] = one
            for d, peer in enumerate(z_peers):
                w3.append(remote(wone, wring.at[z], (w3_send, w3_recv), d, peer))
                w3[-1].start()
            wring[z] = wone[...]
        if s == 6:
            for copy in w3:
                copy.wait_recv()
            for d in FAR_FIRST:
                w4.append(remote(wring, wall_ref.at[side], (w4_send, w4_recv), d, peers[d]))
                w4[-1].start()
            wall_ref[side] = wring[...]
    for copy in others:
        copy.wait()
    mixed = mixes[0].astype(f32)
    for peer in range(1, nmp):
        mixed = mixed + mixes[peer].astype(f32)
    mixed_ref[...] = mixed.astype(bf)
    for half in range(2):
        for way in range(2):
            ring[way, HOPS[way] - 1, half].wait_recv()
    total = down_ref[...] + back[...].astype(f32) + share[z]
    for way in range(2):
        total = total + got[way, HOPS[way] - 1].astype(f32)
    total_ref[...] = total.astype(bf)
    for copy in w4:
        copy.wait()
    for copy in list(ring.values()) + side_copies + w1 + w2 + w3:
        copy.wait_send()


def settle(index, slots, dprior, down, out, weight):
    bf, f32 = jnp.bfloat16, jnp.float32
    nmp = out.shape[0]
    tail = slots.shape[2:]
    block = (ROWS_BLK,) + tail
    piece = weight.shape[1:]
    scratch = [
        (slots.shape, bf),
        ((NZ,) + block, f32),
        ((2, HOPS[0]) + block, bf),
        ((2, HOPS[0]) + block, bf),
        (block, bf),
        (out.shape, bf),
        (weight.shape, bf),
        (piece, bf),
        (piece, bf),
        (piece[1:], f32),
        (piece, f32),
    ]
    sems = pair_sems(2, HOPS[0], 2) + pair_sems(NSIDE - 1) + pair_sems(nmp - 1) + pair_sems(1)
    sems += pair_sems(NSIDE - 1) + pair_sems(NZ - 1) + pair_sems(NZ - 1) + pair_sems(NSIDE - 1)
    return pl.pallas_call(
        functools.partial(settle_kernel, nmp),
        in_specs=[pl.BlockSpec(memory_space=pltpu.SMEM)] + [vmem()] * 5,
        out_specs=[vmem()] * 3,
        out_shape=[
            jax.ShapeDtypeStruct(block, bf),
            jax.ShapeDtypeStruct(out.shape[1:], bf),
            jax.ShapeDtypeStruct(weight.shape, f32),
        ],
        scratch_shapes=[pltpu.VMEM(*shape) for shape in scratch] + sems,
        compiler_params=pltpu.CompilerParams(collective_id=2, has_side_effects=True),
        name="settle",
    )(index, slots, dprior, down, out, weight)


def on_device(
    queries, key_cells, value_cells, out_weight, out_cotangent, parent_rows, window_reach, valid_cells
):
    bf, f32 = jnp.bfloat16, jnp.float32
    features = queries.shape[0]
    heads = features // HEAD_DIM
    width = 2 * features
    x_at, z_at, c_at = (lax.axis_index(name) for name in ROW)
    block_id = (x_at * NZ + z_at) * NC + c_at
    valid = valid_cells[0]
    pairs = jnp.concatenate(
        [key_cells.reshape(heads, HEAD_DIM, -1), value_cells.reshape(heads, HEAD_DIM, -1)], axis=1
    )
    own = pairs.reshape(width, CELLS_BLK).T
    nmp = lax.axis_size("mp")
    wanted = parent_rows.reshape(-1)
    lanes = jnp.concatenate([wanted, valid_cells, jnp.zeros(127 - wanted.shape[0], jnp.int32)])
    info = jnp.broadcast_to(lanes, (8, 128))
    table, asked, cotangents, prior, told = fetch(
        own.reshape(ROWS_BLK, ROW_CELLS, width), info, out_cotangent, nmp
    )
    cotangent_all = cotangents.reshape(-1, CELLS_BLK)
    prior = prior.reshape(CELLS_BLK, width)
    prior_valid = told[0, wanted.shape[0]]
    asked = asked[:, 0, : wanted.shape[0]]
    owner_here = (x_at * NZ + jnp.arange(NZ)) * NC + c_at
    hit = (asked // ROWS_BLK)[:, None, :] == owner_here[None, :, None]
    index = jnp.sum(jnp.where(hit, (asked % ROWS_BLK)[:, None, :], 0), axis=-1)
    side_ids = jnp.arange(NSIDE)
    slot_owner = ((side_ids // NC)[:, None] * NZ + jnp.arange(NZ)[None, :]) * NC + (side_ids % NC)[:, None]
    slot_seen = jnp.any(slot_owner.reshape(-1)[:, None] == (wanted // ROWS_BLK)[None, :], axis=-1)
    cell_ids = jnp.arange(CELLS_BLK)
    prior_seen = (cell_ids < prior_valid) & (window_reach[0] == 1) & (block_id > 0)
    seen = jnp.concatenate([prior_seen, cell_ids < valid, jnp.repeat(slot_seen, ROW_CELLS)])
    seen = seen.astype(f32)[:, None]

    slots = spread(index, table)
    d_attended = jnp.dot(out_weight, cotangent_all, preferred_element_type=f32).astype(bf)
    attended, d_queries, d_prior, d_own, d_slots = attend(
        queries, d_attended, prior, own, slots.reshape(SLOTS * ROW_CELLS, width), seen
    )
    weight_part = lax.dot_general(
        attended, cotangent_all, (((1,), (1,)), ((), ())), preferred_element_type=f32
    )
    pieces = weight_part.astype(bf).reshape(NSIDE, NZ, -1, 128)
    used = pieces.shape[2]
    pieces = jnp.pad(pieces, ((0, 0), (0, 0), (0, SPARE - used), (0, 0)))
    partial_out = lax.dot_general(
        out_weight, attended, (((0,), (0,)), ((), ())), preferred_element_type=f32
    )
    block = (ROWS_BLK, ROW_CELLS, width)
    total, mixed, weight_all = settle(
        index,
        d_slots.reshape(NSIDE, NZ, ROW_CELLS, width),
        d_prior.reshape(block),
        d_own.reshape(block),
        partial_out.astype(bf).reshape(nmp, features, CELLS_BLK),
        pieces,
    )
    weight_grad = weight_all[:, :, :used].reshape(features, -1)
    d_pairs = total.reshape(CELLS_BLK, width).T.reshape(heads, 2, HEAD_DIM, CELLS_BLK)
    d_key_cells = d_pairs[:, 0].reshape(features, CELLS_BLK)
    d_value_cells = d_pairs[:, 1].reshape(features, CELLS_BLK)
    return mixed, d_queries, d_key_cells, d_value_cells, weight_grad


def solution(mesh):
    fine = Mesh(mesh.devices.reshape(NX, NZ, NC, -1), ROW + ("mp",))
    split = P("mp", ROW)
    return jax.shard_map(
        on_device,
        mesh=fine,
        in_specs=(split, split, split, P("mp", None), split, P(ROW, None), P(ROW), P(ROW)),
        out_specs=(split, split, split, split, P("mp", None)),
        check_vma=False,
    )
```

```python
import functools

import jax
import jax.numpy as jnp
from jax import lax
from jax.experimental import pallas as pl
from jax.experimental.pallas import tpu as pltpu
from jax.sharding import Mesh, PartitionSpec as P

HEAD_DIM = 64
CELLS_BLK = 128
ROW_CELLS = 16
ROWS_BLK = 8
NX, NZ, NC = 4, 16, 2
ROW = ("x", "z", "c")
NSIDE = NX * NC
SLOTS = NSIDE * NZ
KEYS = 2 * CELLS_BLK + SLOTS * ROW_CELLS


def attend_kernel(
    q_ref, da_ref, prior_ref, own_ref, slots_ref, seen_ref, att_ref, dq_ref, dprior_ref, down_ref, dslots_ref
):
    scale = HEAD_DIM ** (-0.5)
    kv = jnp.concatenate([prior_ref[...], own_ref[...], slots_ref[...]], axis=0)
    q, da = q_ref[...], da_ref[...]
    blank = jnp.zeros_like(q)
    both = jnp.concatenate(
        [jnp.concatenate([q, blank], axis=1), jnp.concatenate([blank, da], axis=1)], axis=0
    )
    cross = jnp.dot(kv, both, preferred_element_type=jnp.float32)
    visible = seen_ref[...] > 0.5
    scores = jnp.where(visible, cross[:, :CELLS_BLK] * scale, -1e30)
    top = jnp.max(scores, axis=0, keepdims=True)
    grown = jnp.where(visible, jnp.exp(scores - top), 0.0)
    probs = grown / jnp.sum(grown, axis=0, keepdims=True)
    probs_low = probs.astype(jnp.bfloat16)
    d_probs = cross[:, CELLS_BLK:]
    delta = jnp.sum(probs * d_probs, axis=0, keepdims=True)
    d_scores = (probs * (d_probs - delta) * scale).astype(jnp.bfloat16)
    pair = jnp.concatenate([d_scores, probs_low], axis=1)
    d_kv = lax.dot_general(pair, both, (((1,), (1,)), ((), ())), preferred_element_type=jnp.float32)
    mixed = lax.dot_general(kv, pair, (((0,), (0,)), ((), ())), preferred_element_type=jnp.float32)
    dq_ref[...] = mixed[:HEAD_DIM, :CELLS_BLK].astype(jnp.bfloat16)
    att_ref[...] = mixed[HEAD_DIM:, CELLS_BLK:].astype(jnp.bfloat16)
    dprior_ref[...] = d_kv[:CELLS_BLK].astype(jnp.bfloat16)
    down_ref[...] = d_kv[CELLS_BLK : 2 * CELLS_BLK]
    dslots_ref[...] = d_kv[2 * CELLS_BLK :].astype(jnp.bfloat16)


def attend(q, da, prior, own, slots, seen):
    heads = q.shape[0] // HEAD_DIM
    width = own.shape[1]
    feat = pl.BlockSpec((HEAD_DIM, CELLS_BLK), lambda h: (h, 0))
    cells = pl.BlockSpec((CELLS_BLK, 2 * HEAD_DIM), lambda h: (0, h))
    many = pl.BlockSpec((SLOTS * ROW_CELLS, 2 * HEAD_DIM), lambda h: (0, h))
    bf, f32 = jnp.bfloat16, jnp.float32
    return pl.pallas_call(
        attend_kernel,
        grid=(heads,),
        in_specs=[feat, feat, cells, cells, many, pl.BlockSpec((KEYS, 1), lambda h: (0, 0))],
        out_specs=[feat, feat, cells, cells, many],
        out_shape=[
            jax.ShapeDtypeStruct(q.shape, bf),
            jax.ShapeDtypeStruct(q.shape, bf),
            jax.ShapeDtypeStruct((CELLS_BLK, width), bf),
            jax.ShapeDtypeStruct((CELLS_BLK, width), f32),
            jax.ShapeDtypeStruct((SLOTS * ROW_CELLS, width), bf),
        ],
        name="attend",
    )(q, da, prior, own, slots, seen)


MESH = pl.DeviceIdType.MESH
HOPS = (NZ // 2, NZ - NZ // 2 - 1)
HALF = ROWS_BLK // 2
LUMPS = 9


def remote(source, target, sems, spot, device):
    return pltpu.make_async_remote_copy(
        src_ref=source,
        dst_ref=target,
        send_sem=sems[0].at[spot],
        recv_sem=sems[1].at[spot],
        device_id=device,
        device_id_type=MESH,
    )


def step_round(place, distance, size):
    return lax.rem(place + (distance % size), size)


def side_device(side):
    return {"x": lax.div(side, NC), "c": lax.rem(side, NC)}


def line_device(x, z, c, distance):
    line = step_round((x * NZ + z) * NC + c, distance, NX * NZ * NC)
    return {"x": lax.div(line, NZ * NC), "z": lax.rem(lax.div(line, NC), NZ), "c": lax.rem(line, NC)}


def meet(peers):
    barrier = pltpu.get_barrier_semaphore()
    for peer in peers:
        pl.semaphore_signal(barrier, inc=1, device_id=peer, device_id_type=MESH)
    pl.semaphore_wait(barrier, len(peers))


def side_peers(side):
    return [side_device(step_round(side, d, NSIDE)) for d in range(1, NSIDE)]


def fetch_kernel(
    nmp, own_ref, info_ref, cot_ref, table_ref, asked_ref, cots_ref, prior_ref, told_ref,
    ring_send, ring_recv, side_send, side_recv, mp_send, mp_recv, line_send, line_recv,
):
    x, z, c, mp = (lax.axis_index(name) for name in ROW + ("mp",))
    side = x * NC + c
    ways = [{"z": step_round(z, 1, NZ)}, {"z": step_round(z, -1, NZ)}]
    after, before = line_device(x, z, c, 1), line_device(x, z, c, -1)
    mp_peers = [{"mp": step_round(mp, d, nmp)} for d in range(1, nmp)]
    meet(ways + side_peers(side) + mp_peers + [after, before])
    ring = {}

    def hop(way, s, half):
        rows = pl.ds(half * HALF, HALF)
        block = step_round(z, s if way else -s, NZ)
        source = table_ref.at[block, rows] if s else own_ref.at[rows]
        copy = remote(source, table_ref.at[block, rows], (ring_send, ring_recv), (way, s, half), ways[way])
        copy.start()
        ring[way, s, half] = copy

    for half in range(2):
        for way in range(2):
            hop(way, 0, half)
    others = []
    for d, peer in enumerate(side_peers(side)):
        others.append(remote(info_ref, asked_ref.at[side], (side_send, side_recv), d, peer))
    for d, peer in enumerate(mp_peers):
        others.append(remote(cot_ref, cots_ref.at[mp], (mp_send, mp_recv), d, peer))
    others.append(remote(own_ref, prior_ref, (line_send, line_recv), 0, after))
    others.append(remote(info_ref, told_ref, (line_send, line_recv), 1, after))
    for copy in others:
        copy.start()
    table_ref[z] = own_ref[...]
    asked_ref[side] = info_ref[...]
    cots_ref[mp] = cot_ref[...]
    for s in range(1, HOPS[0]):
        for half in range(2):
            for way in range(2):
                if s < HOPS[way]:
                    ring[way, s - 1, half].wait_recv()
                    hop(way, s, half)
    for half in range(2):
        for way in range(2):
            ring[way, HOPS[way] - 1, half].wait_recv()
    for copy in others:
        copy.wait()
    for copy in ring.values():
        copy.wait_send()


def vmem():
    return pl.BlockSpec(memory_space=pltpu.VMEM)


def pair_sems(*shape):
    return [pltpu.SemaphoreType.DMA(shape), pltpu.SemaphoreType.DMA(shape)]


def fetch(own, info, cot, nmp):
    bf, i32 = jnp.bfloat16, jnp.int32
    shapes = [
        ((NZ,) + own.shape, bf),
        ((NSIDE,) + info.shape, i32),
        ((nmp,) + cot.shape, bf),
        (own.shape, bf),
        (info.shape, i32),
    ]
    return pl.pallas_call(
        functools.partial(fetch_kernel, nmp),
        in_specs=[vmem()] * 3,
        out_specs=[vmem()] * 5,
        out_shape=[jax.ShapeDtypeStruct(*shape) for shape in shapes],
        scratch_shapes=pair_sems(2, HOPS[0], 2) + pair_sems(NSIDE - 1) + pair_sems(nmp - 1) + pair_sems(2),
        compiler_params=pltpu.CompilerParams(collective_id=0, has_side_effects=True),
        name="fetch",
    )(own, info, cot)


def spread_kernel(index_ref, table_ref, slots_ref, held, side_send, side_recv):
    side = lax.axis_index("x") * NC + lax.axis_index("c")
    peers = side_peers(side)
    meet(peers)
    copies = []
    for d in FAR_FIRST:
        to = step_round(side, d + 1, NSIDE)
        for z in range(NZ):
            held[d, z] = table_ref[z, index_ref[to, z]]
        copy = remote(held.at[d], slots_ref.at[side], (side_send, side_recv), d, peers[d])
        copy.start()
        copies.append(copy)
    for z in range(NZ):
        slots_ref[side, z] = table_ref[z, index_ref[side, z]]
    for copy in copies:
        copy.wait()


FAR_FIRST = (3, 2, 4, 1, 5, 0, 6)


def spread(index, table):
    tail = table.shape[2:]
    return pl.pallas_call(
        spread_kernel,
        in_specs=[pl.BlockSpec(memory_space=pltpu.SMEM), vmem()],
        out_specs=vmem(),
        out_shape=jax.ShapeDtypeStruct((NSIDE, NZ) + tail, table.dtype),
        scratch_shapes=[pltpu.VMEM((NSIDE - 1, NZ) + tail, table.dtype)] + pair_sems(NSIDE - 1),
        compiler_params=pltpu.CompilerParams(collective_id=1, has_side_effects=True),
        name="spread",
    )(index, table)


def settle_kernel(
    nmp, index_ref, slots_ref, dprior_ref, down_ref, out_ref, weight_ref, total_ref, mixed_ref, wall_ref,
    parts, share, sent, got, back, mixes, wside, wsum, wz, wone, wring,
    ring_send, ring_recv, side_send, side_recv, mp_send, mp_recv, line_send, line_recv,
    w1_send, w1_recv, w2_send, w2_recv, w3_send, w3_recv, w4_send, w4_recv,
):
    bf, f32 = jnp.bfloat16, jnp.float32
    x, z, c, mp = (lax.axis_index(name) for name in ROW + ("mp",))
    side = x * NC + c
    z_peers = [{"z": step_round(z, d, NZ)} for d in range(1, NZ)]
    ways = [z_peers[0], z_peers[-1]]
    after, before = line_device(x, z, c, 1), line_device(x, z, c, -1)
    mp_peers = [{"mp": step_round(mp, d, nmp)} for d in range(1, nmp)]
    peers = side_peers(side)
    meet(z_peers + peers + mp_peers + [after, before])
    side_copies, w1, others = {}, [], []
    order = [spot for s in range(HOPS[0]) for spot in ((NZ // 2 - s), (NZ // 2 + 1 + s) % NZ)]
    for turn, k in enumerate(order):
        t = step_round(z, k, NZ)
        if turn == 4:
            for d in FAR_FIRST:
                to = step_round(side, d + 1, NSIDE)
                w1.append(remote(weight_ref.at[to], wside.at[side], (w1_send, w1_recv), d, peers[d]))
                w1[-1].start()
        for d in FAR_FIRST:
            to = step_round(side, d + 1, NSIDE)
            copy = remote(slots_ref.at[to, t], parts.at[side, t], (side_send, side_recv), (k, d), peers[d])
            copy.start()
            side_copies[k, d] = copy
    for d, peer in enumerate(mp_peers):
        to = step_round(mp, d + 1, nmp)
        others.append(remote(out_ref.at[to], mixes.at[mp], (mp_send, mp_recv), d, peer))
    others.append(remote(dprior_ref, back, (line_send, line_recv), 0, before))
    for copy in others:
        copy.start()
    parts[side] = slots_ref[side]
    wside[side] = weight_ref[side]
    mixes[mp] = out_ref[mp]

    def fill(k):
        t = step_round(z, k, NZ)
        for d in FAR_FIRST:
            side_copies[k, d].wait_recv()
        for row in range(ROWS_BLK):
            total = jnp.zeros(parts.shape[2:], f32)
            for peer in range(NSIDE):
                mark = jnp.where(index_ref[peer, t] == row, 1.0, 0.0)
                total = total + parts[peer, t].astype(f32) * mark
            share[t, row] = total

    ring = {}
    w4 = []
    for s in range(HOPS[0]):
        for k in order[2 * s : 2 * s + 2]:
            fill(k)
        for half in range(2):
            rows = pl.ds(half * HALF, HALF)
            for way in range(2):
                if s >= HOPS[way]:
                    continue
                target = step_round(z, s - HOPS[1] if way else HOPS[0] - s, NZ)
                mine = share[target, rows]
                if s:
                    ring[way, s - 1, half].wait_recv()
                    mine = mine + got[way, s - 1, rows].astype(f32)
                sent[way, s, rows] = mine.astype(bf)
                copy = remote(
                    sent.at[way, s, rows], got.at[way, s, rows], (ring_send, ring_recv), (way, s, half), ways[way]
                )
                copy.start()
                ring[way, s, half] = copy
        if s == 2:
            for copy in w1:
                copy.wait_recv()
            summed = wside[0].astype(f32)
            for peer in range(1, NSIDE):
                summed = summed + wside[peer].astype(f32)
            wsum[...] = summed.astype(bf)
            for d, peer in enumerate(z_peers):
                to = step_round(z, d + 1, NZ)

                @pl.when(to < LUMPS)
                def _():
                    remote(wsum.at[to], wz.at[z], (w2_send, w2_recv), d, peer).start()
        if s == 4:

            @pl.when(z < LUMPS)
            def _():
                for d, peer in enumerate(z_peers):
                    remote(wsum.at[0], wz.at[z], (w2_send, w2_recv), d, peer).wait_recv()
                wz[z] = wsum[z]
                one = wz[0].astype(f32)
                for peer in range(1, NZ):
                    one = one + wz[peer].astype(f32)
                wone[...] = one.astype(bf)
                for d, peer in enumerate(z_peers):
                    remote(wone, wring.at[z], (w3_send, w3_recv), d, peer).start()
                wring[z] = wone[...]
        if s == 7:
            for d, peer in enumerate(z_peers):

                @pl.when(step_round(z, -d - 1, NZ) < LUMPS)
                def _():
                    remote(wone, wring.at[0], (w3_send, w3_recv), d, peer).wait_recv()
            for d in FAR_FIRST:
                w4.append(remote(wring, wall_ref.at[side], (w4_send, w4_recv), d, peers[d]))
                w4[-1].start()
            wall_ref[side] = wring[...]
    for copy in others:
        copy.wait()
    mixed = mixes[0].astype(f32)
    for peer in range(1, nmp):
        mixed = mixed + mixes[peer].astype(f32)
    mixed_ref[...] = mixed.astype(bf)
    for half in range(2):
        for way in range(2):
            ring[way, HOPS[way] - 1, half].wait_recv()
    total = down_ref[...] + back[...].astype(f32) + share[z]
    for way in range(2):
        total = total + got[way, HOPS[way] - 1].astype(f32)
    total_ref[...] = total.astype(bf)
    for copy in w4:
        copy.wait()
    for copy in list(ring.values()) + list(side_copies.values()) + w1:
        copy.wait_send()
    for d, peer in enumerate(z_peers):

        @pl.when(step_round(z, d + 1, NZ) < LUMPS)
        def _():
            remote(wsum.at[0], wz.at[z], (w2_send, w2_recv), d, peer).wait_send()

    @pl.when(z < LUMPS)
    def _():
        for d, peer in enumerate(z_peers):
            remote(wone, wring.at[0], (w3_send, w3_recv), d, peer).wait_send()


def settle(index, slots, dprior, down, out, weight):
    bf, f32 = jnp.bfloat16, jnp.float32
    nmp = out.shape[0]
    tail = slots.shape[2:]
    block = (ROWS_BLK,) + tail
    piece = weight.shape[1:]
    scratch = [
        (slots.shape, bf),
        ((NZ,) + block, f32),
        ((2, HOPS[0]) + block, bf),
        ((2, HOPS[0]) + block, bf),
        (block, bf),
        (out.shape, bf),
        (weight.shape, bf),
        (piece, bf),
        ((NZ,) + piece[1:], bf),
        (piece[1:], bf),
        (piece, bf),
    ]
    sems = pair_sems(2, HOPS[0], 2) + pair_sems(NZ, NSIDE - 1) + pair_sems(nmp - 1) + pair_sems(1)
    sems += pair_sems(NSIDE - 1) + pair_sems(NZ - 1) + pair_sems(NZ - 1) + pair_sems(NSIDE - 1)
    return pl.pallas_call(
        functools.partial(settle_kernel, nmp),
        in_specs=[pl.BlockSpec(memory_space=pltpu.SMEM)] + [vmem()] * 5,
        out_specs=[vmem()] * 3,
        out_shape=[
            jax.ShapeDtypeStruct(block, bf),
            jax.ShapeDtypeStruct(out.shape[1:], bf),
            jax.ShapeDtypeStruct(weight.shape, bf),
        ],
        scratch_shapes=[pltpu.VMEM(*shape) for shape in scratch] + sems,
        compiler_params=pltpu.CompilerParams(collective_id=2, has_side_effects=True),
        name="settle",
    )(index, slots, dprior, down, out, weight)


def on_device(
    queries, key_cells, value_cells, out_weight, out_cotangent, parent_rows, window_reach, valid_cells
):
    bf, f32 = jnp.bfloat16, jnp.float32
    features = queries.shape[0]
    heads = features // HEAD_DIM
    width = 2 * features
    x_at, z_at, c_at = (lax.axis_index(name) for name in ROW)
    block_id = (x_at * NZ + z_at) * NC + c_at
    valid = valid_cells[0]
    pairs = jnp.concatenate(
        [key_cells.reshape(heads, HEAD_DIM, -1), value_cells.reshape(heads, HEAD_DIM, -1)], axis=1
    )
    own = pairs.reshape(width, CELLS_BLK).T
    nmp = lax.axis_size("mp")
    wanted = parent_rows.reshape(-1)
    lanes = jnp.concatenate([wanted, valid_cells, jnp.zeros(127 - wanted.shape[0], jnp.int32)])
    info = jnp.broadcast_to(lanes, (8, 128))
    table, asked, cotangents, prior, told = fetch(
        own.reshape(ROWS_BLK, ROW_CELLS, width), info, out_cotangent, nmp
    )
    cotangent_all = cotangents.reshape(-1, CELLS_BLK)
    prior = prior.reshape(CELLS_BLK, width)
    prior_valid = told[0, wanted.shape[0]]
    asked = asked[:, 0, : wanted.shape[0]]
    owner_here = (x_at * NZ + jnp.arange(NZ)) * NC + c_at
    hit = (asked // ROWS_BLK)[:, None, :] == owner_here[None, :, None]
    index = jnp.sum(jnp.where(hit, (asked % ROWS_BLK)[:, None, :], 0), axis=-1)
    side_ids = jnp.arange(NSIDE)
    slot_owner = ((side_ids // NC)[:, None] * NZ + jnp.arange(NZ)[None, :]) * NC + (side_ids % NC)[:, None]
    slot_seen = jnp.any(slot_owner.reshape(-1)[:, None] == (wanted // ROWS_BLK)[None, :], axis=-1)
    cell_ids = jnp.arange(CELLS_BLK)
    prior_seen = (cell_ids < prior_valid) & (window_reach[0] == 1) & (block_id > 0)
    seen = jnp.concatenate([prior_seen, cell_ids < valid, jnp.repeat(slot_seen, ROW_CELLS)])
    seen = seen.astype(f32)[:, None]

    slots = spread(index, table)
    d_attended = jnp.dot(out_weight, cotangent_all, preferred_element_type=f32).astype(bf)
    attended, d_queries, d_prior, d_own, d_slots = attend(
        queries, d_attended, prior, own, slots.reshape(SLOTS * ROW_CELLS, width), seen
    )
    weight_part = lax.dot_general(
        attended, cotangent_all, (((1,), (1,)), ((), ())), preferred_element_type=f32
    )
    high, wide = features // ROW_CELLS, weight_part.shape[1] // 128
    pieces = weight_part.astype(bf).reshape(high, ROW_CELLS, wide, 128).transpose(0, 2, 1, 3)
    pieces = pieces.reshape(NSIDE, LUMPS, ROW_CELLS, 128)
    partial_out = lax.dot_general(
        out_weight, attended, (((0,), (0,)), ((), ())), preferred_element_type=f32
    )
    block = (ROWS_BLK, ROW_CELLS, width)
    total, mixed, weight_all = settle(
        index,
        d_slots.reshape(NSIDE, NZ, ROW_CELLS, width),
        d_prior.reshape(block),
        d_own.reshape(block),
        partial_out.astype(bf).reshape(nmp, features, CELLS_BLK),
        pieces,
    )
    weight_grad = weight_all.reshape(high, wide, ROW_CELLS, 128).transpose(0, 2, 1, 3)
    weight_grad = weight_grad.reshape(features, -1).astype(f32)
    d_pairs = total.reshape(CELLS_BLK, width).T.reshape(heads, 2, HEAD_DIM, CELLS_BLK)
    d_key_cells = d_pairs[:, 0].reshape(features, CELLS_BLK)
    d_value_cells = d_pairs[:, 1].reshape(features, CELLS_BLK)
    return mixed, d_queries, d_key_cells, d_value_cells, weight_grad


def solution(mesh):
    fine = Mesh(mesh.devices.reshape(NX, NZ, NC, -1), ROW + ("mp",))
    split = P("mp", ROW)
    return jax.shard_map(
        on_device,
        mesh=fine,
        in_specs=(split, split, split, P("mp", None), split, P(ROW, None), P(ROW), P(ROW)),
        out_specs=(split, split, split, split, P("mp", None)),
        check_vma=False,
    )
```

```python
import functools

import jax
import jax.numpy as jnp
from jax import lax
from jax.experimental import pallas as pl
from jax.experimental.pallas import tpu as pltpu
from jax.sharding import Mesh, PartitionSpec as P

HEAD_DIM = 64
CELLS_BLK = 128
ROW_CELLS = 16
ROWS_BLK = 8
NX, NZ, NC = 4, 16, 2
ROW = ("x", "z", "c")
NSIDE = NX * NC
SLOTS = NSIDE * NZ
KEYS = 2 * CELLS_BLK + SLOTS * ROW_CELLS


def attend_kernel(
    q_ref, da_ref, prior_ref, own_ref, slots_ref, seen_ref, att_ref, dq_ref, dprior_ref, down_ref, dslots_ref
):
    scale = HEAD_DIM ** (-0.5)
    kv = jnp.concatenate([prior_ref[...], own_ref[...], slots_ref[...]], axis=0)
    q, da = q_ref[...], da_ref[...]
    blank = jnp.zeros_like(q)
    both = jnp.concatenate(
        [jnp.concatenate([q, blank], axis=1), jnp.concatenate([blank, da], axis=1)], axis=0
    )
    cross = jnp.dot(kv, both, preferred_element_type=jnp.float32)
    visible = seen_ref[...] > 0.5
    scores = jnp.where(visible, cross[:, :CELLS_BLK] * scale, -1e30)
    top = jnp.max(scores, axis=0, keepdims=True)
    grown = jnp.where(visible, jnp.exp(scores - top), 0.0)
    probs = grown / jnp.sum(grown, axis=0, keepdims=True)
    probs_low = probs.astype(jnp.bfloat16)
    d_probs = cross[:, CELLS_BLK:]
    delta = jnp.sum(probs * d_probs, axis=0, keepdims=True)
    d_scores = (probs * (d_probs - delta) * scale).astype(jnp.bfloat16)
    pair = jnp.concatenate([d_scores, probs_low], axis=1)
    d_kv = lax.dot_general(pair, both, (((1,), (1,)), ((), ())), preferred_element_type=jnp.float32)
    mixed = lax.dot_general(kv, pair, (((0,), (0,)), ((), ())), preferred_element_type=jnp.float32)
    dq_ref[...] = mixed[:HEAD_DIM, :CELLS_BLK].astype(jnp.bfloat16)
    att_ref[...] = mixed[HEAD_DIM:, CELLS_BLK:].astype(jnp.bfloat16)
    dprior_ref[...] = d_kv[:CELLS_BLK].astype(jnp.bfloat16)
    down_ref[...] = d_kv[CELLS_BLK : 2 * CELLS_BLK]
    dslots_ref[...] = d_kv[2 * CELLS_BLK :].astype(jnp.bfloat16)


def attend(q, da, prior, own, slots, seen):
    heads = q.shape[0] // HEAD_DIM
    width = own.shape[1]
    feat = pl.BlockSpec((HEAD_DIM, CELLS_BLK), lambda h: (h, 0))
    cells = pl.BlockSpec((CELLS_BLK, 2 * HEAD_DIM), lambda h: (0, h))
    many = pl.BlockSpec((SLOTS * ROW_CELLS, 2 * HEAD_DIM), lambda h: (0, h))
    bf, f32 = jnp.bfloat16, jnp.float32
    return pl.pallas_call(
        attend_kernel,
        grid=(heads,),
        in_specs=[feat, feat, cells, cells, many, pl.BlockSpec((KEYS, 1), lambda h: (0, 0))],
        out_specs=[feat, feat, cells, cells, many],
        out_shape=[
            jax.ShapeDtypeStruct(q.shape, bf),
            jax.ShapeDtypeStruct(q.shape, bf),
            jax.ShapeDtypeStruct((CELLS_BLK, width), bf),
            jax.ShapeDtypeStruct((CELLS_BLK, width), f32),
            jax.ShapeDtypeStruct((SLOTS * ROW_CELLS, width), bf),
        ],
        name="attend",
    )(q, da, prior, own, slots, seen)


MESH = pl.DeviceIdType.MESH
HOPS = (NZ // 2, NZ - NZ // 2 - 1)
HALF = ROWS_BLK // 2
LUMPS = 9


def remote(source, target, sems, spot, device):
    return pltpu.make_async_remote_copy(
        src_ref=source,
        dst_ref=target,
        send_sem=sems[0].at[spot],
        recv_sem=sems[1].at[spot],
        device_id=device,
        device_id_type=MESH,
    )


def step_round(place, distance, size):
    return lax.rem(place + (distance % size), size)


def side_device(side):
    return {"x": lax.div(side, NC), "c": lax.rem(side, NC)}


def line_device(x, z, c, distance):
    line = step_round((x * NZ + z) * NC + c, distance, NX * NZ * NC)
    return {"x": lax.div(line, NZ * NC), "z": lax.rem(lax.div(line, NC), NZ), "c": lax.rem(line, NC)}


def meet(peers):
    barrier = pltpu.get_barrier_semaphore()
    for peer in peers:
        pl.semaphore_signal(barrier, inc=1, device_id=peer, device_id_type=MESH)
    pl.semaphore_wait(barrier, len(peers))


def side_peers(side):
    return [side_device(step_round(side, d, NSIDE)) for d in range(1, NSIDE)]


FAR_FIRST = (3, 2, 4, 1, 5, 0, 6)


def fetch_kernel(
    nmp, fanout, own_ref, info_ref, cot_ref, slots_ref, index_ref, cots_ref, prior_ref, told_ref,
    table, asked, held, ready, spots,
    ring_send, ring_recv, info_send, info_recv, side_send, side_recv, mp_send, mp_recv, line_send, line_recv, spots_sem,
):
    x, z, c, mp = (lax.axis_index(name) for name in ROW + ("mp",))
    side = x * NC + c
    ways = [{"z": step_round(z, 1, NZ)}, {"z": step_round(z, -1, NZ)}]
    after, before = line_device(x, z, c, 1), line_device(x, z, c, -1)
    mp_peers = [{"mp": step_round(mp, d, nmp)} for d in range(1, nmp)]
    peers = side_peers(side)
    meet(ways + peers + mp_peers + [after, before])
    ring, picked = {}, {}

    def hop(way, s, half):
        rows = pl.ds(half * HALF, HALF)
        block = step_round(z, s if way else -s, NZ)
        source = table.at[block, rows] if s else own_ref.at[rows]
        copy = remote(source, table.at[block, rows], (ring_send, ring_recv), (way, s, half), ways[way])
        copy.start()
        ring[way, s, half] = copy

    def pick(distance):
        block, k = step_round(z, distance, NZ), distance % NZ
        ready[...] = table[block]
        for d in FAR_FIRST:
            to = step_round(side, d + 1, NSIDE)
            held[d, block] = ready[spots[block, to]]
            copy = remote(held.at[d, block], slots_ref.at[side, block], (side_send, side_recv), (k, d), peers[d])
            copy.start()
            picked[k, d] = copy
        slots_ref[side, block] = ready[spots[block, side]]

    infos = [remote(info_ref, asked.at[side], (info_send, info_recv), d, peers[d]) for d in FAR_FIRST]
    for copy in infos:
        copy.start()
    for half in range(2):
        for way in range(2):
            hop(way, 0, half)
    others = []
    for d, peer in enumerate(mp_peers):
        others.append(remote(cot_ref, cots_ref.at[mp], (mp_send, mp_recv), d, peer))
        others[-1].start()
    table[z] = own_ref[...]
    asked[side] = info_ref[...]
    cots_ref[mp] = cot_ref[...]
    for copy in infos:
        copy.wait_recv()
    shape = (NZ, 128)
    owner = (x * NZ + lax.broadcasted_iota(jnp.int32, shape, 0)) * NC + c
    lane = lax.broadcasted_iota(jnp.int32, shape, 1)
    found = jnp.zeros(shape, jnp.int32)
    for peer in range(NSIDE):
        wanted = jnp.concatenate([asked[peer]] * (NZ // 8), axis=0)
        hit = (lax.shift_right_logical(wanted, 3) == owner) & (lane < fanout)
        local = jnp.sum(jnp.where(hit, wanted & 7, 0), axis=1, keepdims=True)
        found = jnp.where(lane == peer, local, found)
    index_ref[...] = found
    local_copy = pltpu.make_async_copy(index_ref, spots, spots_sem.at[0])
    local_copy.start()
    local_copy.wait()
    pick(0)
    for s in range(1, HOPS[0] + 1):
        for half in range(2):
            for way in range(2):
                if s <= HOPS[way]:
                    ring[way, s - 1, half].wait_recv()
                if s < HOPS[way]:
                    hop(way, s, half)
        if s == 5:
            others.append(remote(own_ref, prior_ref, (line_send, line_recv), 0, after))
            others.append(remote(info_ref, told_ref, (line_send, line_recv), 1, after))
            for copy in others[-2:]:
                copy.start()
        for way in range(2):
            if s <= HOPS[way]:
                pick(s if way else -s)
    for copy in others:
        copy.wait()
    for copy in picked.values():
        copy.wait()
    for copy in list(ring.values()) + infos:
        copy.wait_send()


def vmem():
    return pl.BlockSpec(memory_space=pltpu.VMEM)


def pair_sems(*shape):
    return [pltpu.SemaphoreType.DMA(shape), pltpu.SemaphoreType.DMA(shape)]


def fetch(own, info, cot, nmp, fanout):
    bf, i32 = jnp.bfloat16, jnp.int32
    tail = own.shape[1:]
    shapes = [
        ((NSIDE, NZ) + tail, bf),
        ((NZ, 128), i32),
        ((nmp,) + cot.shape, bf),
        (own.shape, bf),
        (info.shape, i32),
    ]
    scratch = [
        pltpu.VMEM((NZ,) + own.shape, bf),
        pltpu.VMEM((NSIDE,) + info.shape, i32),
        pltpu.VMEM((NSIDE - 1, NZ) + tail, bf),
        pltpu.VMEM(own.shape, bf),
        pltpu.SMEM((NZ, 128), i32),
    ]
    sems = pair_sems(2, HOPS[0], 2) + pair_sems(NSIDE - 1) + pair_sems(NZ, NSIDE - 1)
    sems += pair_sems(nmp - 1) + pair_sems(2) + [pltpu.SemaphoreType.DMA((1,))]
    return pl.pallas_call(
        functools.partial(fetch_kernel, nmp, fanout),
        in_specs=[vmem()] * 3,
        out_specs=[vmem()] * 5,
        out_shape=[jax.ShapeDtypeStruct(*shape) for shape in shapes],
        scratch_shapes=scratch + sems,
        compiler_params=pltpu.CompilerParams(collective_id=0, has_side_effects=True),
        name="fetch",
    )(own, info, cot)


def settle_kernel(
    nmp, index_ref, slots_ref, dprior_ref, down_ref, out_ref, weight_ref, total_ref, mixed_ref, wall_ref,
    parts, share, sent, got, back, mixes, wside, wsum, wz, wone, wring,
    ring_send, ring_recv, side_send, side_recv, mp_send, mp_recv, line_send, line_recv,
    w1_send, w1_recv, w2_send, w2_recv, w3_send, w3_recv, w4_send, w4_recv,
):
    bf, f32 = jnp.bfloat16, jnp.float32
    x, z, c, mp = (lax.axis_index(name) for name in ROW + ("mp",))
    side = x * NC + c
    z_peers = [{"z": step_round(z, d, NZ)} for d in range(1, NZ)]
    ways = [z_peers[0], z_peers[-1]]
    after, before = line_device(x, z, c, 1), line_device(x, z, c, -1)
    mp_peers = [{"mp": step_round(mp, d, nmp)} for d in range(1, nmp)]
    peers = side_peers(side)
    meet(z_peers + peers + mp_peers + [after, before])
    side_copies, w1, others = {}, [], []
    order = [spot for s in range(HOPS[0]) for spot in ((NZ // 2 - s), (NZ // 2 + 1 + s) % NZ)]
    for turn, k in enumerate(order):
        t = step_round(z, k, NZ)
        if turn == 4:
            for d in FAR_FIRST:
                to = step_round(side, d + 1, NSIDE)
                w1.append(remote(weight_ref.at[to], wside.at[side], (w1_send, w1_recv), d, peers[d]))
                w1[-1].start()
        for d in FAR_FIRST:
            to = step_round(side, d + 1, NSIDE)
            copy = remote(slots_ref.at[to, t], parts.at[side, t], (side_send, side_recv), (k, d), peers[d])
            copy.start()
            side_copies[k, d] = copy
    for d, peer in enumerate(mp_peers):
        to = step_round(mp, d + 1, nmp)
        others.append(remote(out_ref.at[to], mixes.at[mp], (mp_send, mp_recv), d, peer))
    others.append(remote(dprior_ref, back, (line_send, line_recv), 0, before))
    for copy in others:
        copy.start()
    parts[side] = slots_ref[side]
    wside[side] = weight_ref[side]
    mixes[mp] = out_ref[mp]

    def fill(k):
        t = step_round(z, k, NZ)
        for d in FAR_FIRST:
            side_copies[k, d].wait_recv()
        for row in range(ROWS_BLK):
            total = jnp.zeros(parts.shape[2:], f32)
            for peer in range(NSIDE):
                mark = jnp.where(index_ref[t, peer] == row, 1.0, 0.0)
                total = total + parts[peer, t].astype(f32) * mark
            share[t, row] = total

    ring = {}
    w4 = []
    for s in range(HOPS[0]):
        for k in order[2 * s : 2 * s + 2]:
            fill(k)
        for half in range(2):
            rows = pl.ds(half * HALF, HALF)
            for way in range(2):
                if s >= HOPS[way]:
                    continue
                target = step_round(z, s - HOPS[1] if way else HOPS[0] - s, NZ)
                mine = share[target, rows]
                if s:
                    ring[way, s - 1, half].wait_recv()
                    mine = mine + got[way, s - 1, rows].astype(f32)
                sent[way, s, rows] = mine.astype(bf)
                copy = remote(
                    sent.at[way, s, rows], got.at[way, s, rows], (ring_send, ring_recv), (way, s, half), ways[way]
                )
                copy.start()
                ring[way, s, half] = copy
        if s == 2:
            for copy in w1:
                copy.wait_recv()
            summed = wside[0].astype(f32)
            for peer in range(1, NSIDE):
                summed = summed + wside[peer].astype(f32)
            wsum[...] = summed.astype(bf)
            for d, peer in enumerate(z_peers):
                to = step_round(z, d + 1, NZ)

                @pl.when(to < LUMPS)
                def _():
                    remote(wsum.at[to], wz.at[z], (w2_send, w2_recv), d, peer).start()
        if s == 4:

            @pl.when(z < LUMPS)
            def _():
                for d, peer in enumerate(z_peers):
                    remote(wsum.at[0], wz.at[z], (w2_send, w2_recv), d, peer).wait_recv()
                wz[z] = wsum[z]
                one = wz[0].astype(f32)
                for peer in range(1, NZ):
                    one = one + wz[peer].astype(f32)
                wone[...] = one.astype(bf)
                for d, peer in enumerate(z_peers):
                    remote(wone, wring.at[z], (w3_send, w3_recv), d, peer).start()
                wring[z] = wone[...]
        if s == 7:
            for d, peer in enumerate(z_peers):

                @pl.when(step_round(z, -d - 1, NZ) < LUMPS)
                def _():
                    remote(wone, wring.at[0], (w3_send, w3_recv), d, peer).wait_recv()
            for d in FAR_FIRST:
                w4.append(remote(wring, wall_ref.at[side], (w4_send, w4_recv), d, peers[d]))
                w4[-1].start()
            wall_ref[side] = wring[...]
    for copy in others:
        copy.wait()
    mixed = mixes[0].astype(f32)
    for peer in range(1, nmp):
        mixed = mixed + mixes[peer].astype(f32)
    mixed_ref[...] = mixed.astype(bf)
    for half in range(2):
        for way in range(2):
            ring[way, HOPS[way] - 1, half].wait_recv()
    total = down_ref[...] + back[...].astype(f32) + share[z]
    for way in range(2):
        total = total + got[way, HOPS[way] - 1].astype(f32)
    total_ref[...] = total.astype(bf)
    for copy in w4:
        copy.wait()
    for copy in list(ring.values()) + list(side_copies.values()) + w1:
        copy.wait_send()
    for d, peer in enumerate(z_peers):

        @pl.when(step_round(z, d + 1, NZ) < LUMPS)
        def _():
            remote(wsum.at[0], wz.at[z], (w2_send, w2_recv), d, peer).wait_send()

    @pl.when(z < LUMPS)
    def _():
        for d, peer in enumerate(z_peers):
            remote(wone, wring.at[0], (w3_send, w3_recv), d, peer).wait_send()


def settle(index, slots, dprior, down, out, weight):
    bf, f32 = jnp.bfloat16, jnp.float32
    nmp = out.shape[0]
    tail = slots.shape[2:]
    block = (ROWS_BLK,) + tail
    piece = weight.shape[1:]
    scratch = [
        (slots.shape, bf),
        ((NZ,) + block, f32),
        ((2, HOPS[0]) + block, bf),
        ((2, HOPS[0]) + block, bf),
        (block, bf),
        (out.shape, bf),
        (weight.shape, bf),
        (piece, bf),
        ((NZ,) + piece[1:], bf),
        (piece[1:], bf),
        (piece, bf),
    ]
    sems = pair_sems(2, HOPS[0], 2) + pair_sems(NZ, NSIDE - 1) + pair_sems(nmp - 1) + pair_sems(1)
    sems += pair_sems(NSIDE - 1) + pair_sems(NZ - 1) + pair_sems(NZ - 1) + pair_sems(NSIDE - 1)
    return pl.pallas_call(
        functools.partial(settle_kernel, nmp),
        in_specs=[pl.BlockSpec(memory_space=pltpu.SMEM)] + [vmem()] * 5,
        out_specs=[vmem()] * 3,
        out_shape=[
            jax.ShapeDtypeStruct(block, bf),
            jax.ShapeDtypeStruct(out.shape[1:], bf),
            jax.ShapeDtypeStruct(weight.shape, bf),
        ],
        scratch_shapes=[pltpu.VMEM(*shape) for shape in scratch] + sems,
        compiler_params=pltpu.CompilerParams(collective_id=1, has_side_effects=True),
        name="settle",
    )(index, slots, dprior, down, out, weight)


def on_device(
    queries, key_cells, value_cells, out_weight, out_cotangent, parent_rows, window_reach, valid_cells
):
    bf, f32 = jnp.bfloat16, jnp.float32
    features = queries.shape[0]
    heads = features // HEAD_DIM
    width = 2 * features
    x_at, z_at, c_at = (lax.axis_index(name) for name in ROW)
    block_id = (x_at * NZ + z_at) * NC + c_at
    valid = valid_cells[0]
    pairs = jnp.concatenate(
        [key_cells.reshape(heads, HEAD_DIM, -1), value_cells.reshape(heads, HEAD_DIM, -1)], axis=1
    )
    own = pairs.reshape(width, CELLS_BLK).T
    nmp = lax.axis_size("mp")
    wanted = parent_rows.reshape(-1)
    lanes = jnp.concatenate([wanted, valid_cells, jnp.zeros(127 - wanted.shape[0], jnp.int32)])
    info = jnp.broadcast_to(lanes, (8, 128))
    slots, index, cotangents, prior, told = fetch(
        own.reshape(ROWS_BLK, ROW_CELLS, width), info, out_cotangent, nmp, wanted.shape[0]
    )
    cotangent_all = cotangents.reshape(-1, CELLS_BLK)
    prior = prior.reshape(CELLS_BLK, width)
    prior_valid = told[0, wanted.shape[0]]
    side_ids = jnp.arange(NSIDE)
    slot_owner = ((side_ids // NC)[:, None] * NZ + jnp.arange(NZ)[None, :]) * NC + (side_ids % NC)[:, None]
    slot_seen = jnp.any(slot_owner.reshape(-1)[:, None] == (wanted // ROWS_BLK)[None, :], axis=-1)
    cell_ids = jnp.arange(CELLS_BLK)
    prior_seen = (cell_ids < prior_valid) & (window_reach[0] == 1) & (block_id > 0)
    seen = jnp.concatenate([prior_seen, cell_ids < valid, jnp.repeat(slot_seen, ROW_CELLS)])
    seen = seen.astype(f32)[:, None]

    d_attended = jnp.dot(out_weight, cotangent_all, preferred_element_type=f32).astype(bf)
    attended, d_queries, d_prior, d_own, d_slots = attend(
        queries, d_attended, prior, own, slots.reshape(SLOTS * ROW_CELLS, width), seen
    )
    weight_part = lax.dot_general(
        attended, cotangent_all, (((1,), (1,)), ((), ())), preferred_element_type=f32
    )
    high, wide = features // ROW_CELLS, weight_part.shape[1] // 128
    pieces = weight_part.astype(bf).reshape(high, ROW_CELLS, wide, 128).transpose(0, 2, 1, 3)
    pieces = pieces.reshape(NSIDE, LUMPS, ROW_CELLS, 128)
    partial_out = lax.dot_general(
        out_weight, attended, (((0,), (0,)), ((), ())), preferred_element_type=f32
    )
    block = (ROWS_BLK, ROW_CELLS, width)
    total, mixed, weight_all = settle(
        index,
        d_slots.reshape(NSIDE, NZ, ROW_CELLS, width),
        d_prior.reshape(block),
        d_own.reshape(block),
        partial_out.astype(bf).reshape(nmp, features, CELLS_BLK),
        pieces,
    )
    weight_grad = weight_all.reshape(high, wide, ROW_CELLS, 128).transpose(0, 2, 1, 3)
    weight_grad = weight_grad.reshape(features, -1).astype(f32)
    d_pairs = total.reshape(CELLS_BLK, width).T.reshape(heads, 2, HEAD_DIM, CELLS_BLK)
    d_key_cells = d_pairs[:, 0].reshape(features, CELLS_BLK)
    d_value_cells = d_pairs[:, 1].reshape(features, CELLS_BLK)
    return mixed, d_queries, d_key_cells, d_value_cells, weight_grad


def solution(mesh):
    fine = Mesh(mesh.devices.reshape(NX, NZ, NC, -1), ROW + ("mp",))
    split = P("mp", ROW)
    return jax.shard_map(
        on_device,
        mesh=fine,
        in_specs=(split, split, split, P("mp", None), split, P(ROW, None), P(ROW), P(ROW)),
        out_specs=(split, split, split, split, P("mp", None)),
        check_vma=False,
    )
```

```python
import functools

import jax
import jax.numpy as jnp
from jax import lax
from jax.experimental import pallas as pl
from jax.experimental.pallas import tpu as pltpu
from jax.sharding import Mesh, PartitionSpec as P

HEAD_DIM = 64
CELLS_BLK = 128
ROW_CELLS = 16
ROWS_BLK = 8
NX, NZ, NC = 4, 16, 2
ROW = ("x", "z", "c")
NSIDE = NX * NC
SLOTS = NSIDE * NZ
KEYS = 2 * CELLS_BLK + SLOTS * ROW_CELLS


def attend(q, da, kv, visible):
    scale = HEAD_DIM ** (-0.5)
    blank = jnp.zeros_like(q)
    both = jnp.concatenate(
        [jnp.concatenate([q, blank], axis=1), jnp.concatenate([blank, da], axis=1)], axis=0
    )
    cross = jnp.dot(kv, both, preferred_element_type=jnp.float32)
    scores = jnp.where(visible, cross[:, :CELLS_BLK] * scale, -1e30)
    top = jnp.max(scores, axis=0, keepdims=True)
    grown = jnp.where(visible, jnp.exp(scores - top), 0.0)
    probs = grown / jnp.sum(grown, axis=0, keepdims=True)
    probs_low = probs.astype(jnp.bfloat16)
    d_probs = cross[:, CELLS_BLK:]
    delta = jnp.sum(probs * d_probs, axis=0, keepdims=True)
    d_scores = (probs * (d_probs - delta) * scale).astype(jnp.bfloat16)
    pair = jnp.concatenate([d_scores, probs_low], axis=1)
    d_kv = lax.dot_general(pair, both, (((1,), (1,)), ((), ())), preferred_element_type=jnp.float32)
    mixed = lax.dot_general(kv, pair, (((0,), (0,)), ((), ())), preferred_element_type=jnp.float32)
    return d_kv, mixed[:HEAD_DIM, :CELLS_BLK], mixed[HEAD_DIM:, CELLS_BLK:]


MESH = pl.DeviceIdType.MESH
HOPS = (NZ // 2, NZ - NZ // 2 - 1)
HALF = ROWS_BLK // 2
LUMPS = 9


def remote(source, target, sems, spot, device):
    return pltpu.make_async_remote_copy(
        src_ref=source,
        dst_ref=target,
        send_sem=sems[0].at[spot],
        recv_sem=sems[1].at[spot],
        device_id=device,
        device_id_type=MESH,
    )


def step_round(place, distance, size):
    return lax.rem(place + (distance % size), size)


def side_device(side):
    return {"x": lax.div(side, NC), "c": lax.rem(side, NC)}


def line_device(x, z, c, distance):
    line = step_round((x * NZ + z) * NC + c, distance, NX * NZ * NC)
    return {"x": lax.div(line, NZ * NC), "z": lax.rem(lax.div(line, NC), NZ), "c": lax.rem(line, NC)}


def meet(peers):
    barrier = pltpu.get_barrier_semaphore()
    for peer in peers:
        pl.semaphore_signal(barrier, inc=1, device_id=peer, device_id_type=MESH)
    pl.semaphore_wait(barrier, len(peers))


def side_peers(side):
    return [side_device(step_round(side, d, NSIDE)) for d in range(1, NSIDE)]


FAR_FIRST = (3, 2, 4, 1, 5, 0, 6)


def fetch_kernel(
    nmp, fanout, own_ref, info_ref, cot_ref, slots_ref, index_ref, cots_ref, prior_ref, told_ref,
    table, asked, held, ready, spots,
    ring_send, ring_recv, info_send, info_recv, side_send, side_recv, mp_send, mp_recv, line_send, line_recv, spots_sem,
):
    x, z, c, mp = (lax.axis_index(name) for name in ROW + ("mp",))
    side = x * NC + c
    ways = [{"z": step_round(z, 1, NZ)}, {"z": step_round(z, -1, NZ)}]
    after, before = line_device(x, z, c, 1), line_device(x, z, c, -1)
    mp_peers = [{"mp": step_round(mp, d, nmp)} for d in range(1, nmp)]
    peers = side_peers(side)
    meet(ways + peers + mp_peers + [after, before])
    ring, picked = {}, {}

    def hop(way, s, half):
        rows = pl.ds(half * HALF, HALF)
        block = step_round(z, s if way else -s, NZ)
        source = table.at[block, rows] if s else own_ref.at[rows]
        copy = remote(source, table.at[block, rows], (ring_send, ring_recv), (way, s, half), ways[way])
        copy.start()
        ring[way, s, half] = copy

    def pick(distance):
        block, k = step_round(z, distance, NZ), distance % NZ
        ready[...] = table[block]
        for d in FAR_FIRST:
            to = step_round(side, d + 1, NSIDE)
            held[d, block] = ready[spots[block, to]]
            copy = remote(held.at[d, block], slots_ref.at[side, block], (side_send, side_recv), (k, d), peers[d])
            copy.start()
            picked[k, d] = copy
        slots_ref[side, block] = ready[spots[block, side]]

    infos = [remote(info_ref, asked.at[side], (info_send, info_recv), d, peers[d]) for d in FAR_FIRST]
    for copy in infos:
        copy.start()
    for half in range(2):
        for way in range(2):
            hop(way, 0, half)
    others = []
    for d, peer in enumerate(mp_peers):
        others.append(remote(cot_ref, cots_ref.at[mp], (mp_send, mp_recv), d, peer))
        others[-1].start()
    table[z] = own_ref[...]
    asked[side] = info_ref[...]
    cots_ref[mp] = cot_ref[...]
    for copy in infos:
        copy.wait_recv()
    shape = (NZ, 128)
    owner = (x * NZ + lax.broadcasted_iota(jnp.int32, shape, 0)) * NC + c
    lane = lax.broadcasted_iota(jnp.int32, shape, 1)
    found = jnp.zeros(shape, jnp.int32)
    for peer in range(NSIDE):
        wanted = jnp.concatenate([asked[peer]] * (NZ // 8), axis=0)
        hit = (lax.shift_right_logical(wanted, 3) == owner) & (lane < fanout)
        local = jnp.sum(jnp.where(hit, wanted & 7, 0), axis=1, keepdims=True)
        found = jnp.where(lane == peer, local, found)
    index_ref[...] = found
    local_copy = pltpu.make_async_copy(index_ref, spots, spots_sem.at[0])
    local_copy.start()
    local_copy.wait()
    pick(0)
    for s in range(1, HOPS[0] + 1):
        for half in range(2):
            for way in range(2):
                if s <= HOPS[way]:
                    ring[way, s - 1, half].wait_recv()
                if s < HOPS[way]:
                    hop(way, s, half)
        if s == 5:
            others.append(remote(own_ref, prior_ref, (line_send, line_recv), 0, after))
            others.append(remote(info_ref, told_ref, (line_send, line_recv), 1, after))
            for copy in others[-2:]:
                copy.start()
        for way in range(2):
            if s <= HOPS[way]:
                pick(s if way else -s)
    for copy in others:
        copy.wait()
    for copy in picked.values():
        copy.wait()
    for copy in list(ring.values()) + infos:
        copy.wait_send()


def vmem():
    return pl.BlockSpec(memory_space=pltpu.VMEM)


def pair_sems(*shape):
    return [pltpu.SemaphoreType.DMA(shape), pltpu.SemaphoreType.DMA(shape)]


def fetch(own, info, cot, nmp, fanout):
    bf, i32 = jnp.bfloat16, jnp.int32
    tail = own.shape[1:]
    shapes = [
        ((NSIDE, NZ) + tail, bf),
        ((NZ, 128), i32),
        ((nmp,) + cot.shape, bf),
        (own.shape, bf),
        (info.shape, i32),
    ]
    scratch = [
        pltpu.VMEM((NZ,) + own.shape, bf),
        pltpu.VMEM((NSIDE,) + info.shape, i32),
        pltpu.VMEM((NSIDE - 1, NZ) + tail, bf),
        pltpu.VMEM(own.shape, bf),
        pltpu.SMEM((NZ, 128), i32),
    ]
    sems = pair_sems(2, HOPS[0], 2) + pair_sems(NSIDE - 1) + pair_sems(NZ, NSIDE - 1)
    sems += pair_sems(nmp - 1) + pair_sems(2) + [pltpu.SemaphoreType.DMA((1,))]
    return pl.pallas_call(
        functools.partial(fetch_kernel, nmp, fanout),
        in_specs=[vmem()] * 3,
        out_specs=[vmem()] * 5,
        out_shape=[jax.ShapeDtypeStruct(*shape) for shape in shapes],
        scratch_shapes=scratch + sems,
        compiler_params=pltpu.CompilerParams(collective_id=0, has_side_effects=True),
        name="fetch",
    )(own, info, cot)


def settle_kernel(
    nmp, index_ref, q_ref, da_ref, prior_ref, own_ref, keys_ref, seen_ref, proj_ref, cot_ref,
    total_ref, mixed_ref, dq_ref, wall_ref,
    slots_ref, dprior_ref, down_ref, att_ref, out_ref, weight_ref,
    parts, share, sent, got, back, mixes, wside, wsum, wz, wone, wring,
    ring_send, ring_recv, side_send, side_recv, mp_send, mp_recv, line_send, line_recv,
    w1_send, w1_recv, w2_send, w2_recv, w3_send, w3_recv, w4_send, w4_recv,
):
    bf, f32 = jnp.bfloat16, jnp.float32
    x, z, c, mp = (lax.axis_index(name) for name in ROW + ("mp",))
    side = x * NC + c
    z_peers = [{"z": step_round(z, d, NZ)} for d in range(1, NZ)]
    ways = [z_peers[0], z_peers[-1]]
    after, before = line_device(x, z, c, 1), line_device(x, z, c, -1)
    mp_peers = [{"mp": step_round(mp, d, nmp)} for d in range(1, nmp)]
    peers = side_peers(side)
    everyone = z_peers + peers + mp_peers + [after, before]
    barrier = pltpu.get_barrier_semaphore()
    for peer in everyone:
        pl.semaphore_signal(barrier, inc=1, device_id=peer, device_id_type=MESH)
    visible = seen_ref[...] > 0.5
    for head in range(q_ref.shape[0] // HEAD_DIM):
        feats = slice(head * HEAD_DIM, (head + 1) * HEAD_DIM)
        cols = slice(head * 2 * HEAD_DIM, (head + 1) * 2 * HEAD_DIM)
        kv = jnp.concatenate([prior_ref[:, cols], own_ref[:, cols], keys_ref[:, cols]], axis=0)
        d_kv, dq, att = attend(q_ref[feats, :], da_ref[feats, :], kv, visible)
        dq_ref[feats, :] = dq.astype(bf)
        att_ref[feats, :] = att.astype(bf)
        block = (ROWS_BLK, ROW_CELLS, 2 * HEAD_DIM)
        dprior_ref[:, :, cols] = d_kv[:CELLS_BLK].astype(bf).reshape(block)
        down_ref[:, :, cols] = d_kv[CELLS_BLK : 2 * CELLS_BLK].reshape(block)
        slots_ref[:, :, :, cols] = d_kv[2 * CELLS_BLK :].astype(bf).reshape((NSIDE, NZ) + block[1:])
    attended = att_ref[...]
    out = lax.dot_general(proj_ref[...], attended, (((0,), (0,)), ((), ())), preferred_element_type=f32)
    out_ref[...] = out.astype(bf).reshape(out_ref.shape)
    weight = lax.dot_general(attended, cot_ref[...], (((1,), (1,)), ((), ())), preferred_element_type=f32)
    weight = weight.astype(bf)
    wide = weight.shape[1] // 128
    for tile in range(NSIDE * LUMPS):
        row, col = tile // wide * ROW_CELLS, tile % wide * 128
        weight_ref[tile // LUMPS, tile % LUMPS] = weight[row : row + ROW_CELLS, col : col + 128]
    pl.semaphore_wait(barrier, len(everyone))
    side_copies, w1, others = {}, [], []
    order = [spot for s in range(HOPS[0]) for spot in ((NZ // 2 - s), (NZ // 2 + 1 + s) % NZ)]
    for turn, k in enumerate(order):
        t = step_round(z, k, NZ)
        if turn == 4:
            for d in FAR_FIRST:
                to = step_round(side, d + 1, NSIDE)
                w1.append(remote(weight_ref.at[to], wside.at[side], (w1_send, w1_recv), d, peers[d]))
                w1[-1].start()
        for d in FAR_FIRST:
            to = step_round(side, d + 1, NSIDE)
            copy = remote(slots_ref.at[to, t], parts.at[side, t], (side_send, side_recv), (k, d), peers[d])
            copy.start()
            side_copies[k, d] = copy
    for d, peer in enumerate(mp_peers):
        to = step_round(mp, d + 1, nmp)
        others.append(remote(out_ref.at[to], mixes.at[mp], (mp_send, mp_recv), d, peer))
    others.append(remote(dprior_ref, back, (line_send, line_recv), 0, before))
    for copy in others:
        copy.start()
    parts[side] = slots_ref[side]
    wside[side] = weight_ref[side]
    mixes[mp] = out_ref[mp]

    def fill(k):
        t = step_round(z, k, NZ)
        for d in FAR_FIRST:
            side_copies[k, d].wait_recv()
        for row in range(ROWS_BLK):
            total = jnp.zeros(parts.shape[2:], f32)
            for peer in range(NSIDE):
                mark = jnp.where(index_ref[t, peer] == row, 1.0, 0.0)
                total = total + parts[peer, t].astype(f32) * mark
            share[t, row] = total

    ring = {}
    w4 = []
    for s in range(HOPS[0]):
        for k in order[2 * s : 2 * s + 2]:
            fill(k)
        for half in range(2):
            rows = pl.ds(half * HALF, HALF)
            for way in range(2):
                if s >= HOPS[way]:
                    continue
                target = step_round(z, s - HOPS[1] if way else HOPS[0] - s, NZ)
                mine = share[target, rows]
                if s:
                    ring[way, s - 1, half].wait_recv()
                    mine = mine + got[way, s - 1, rows].astype(f32)
                sent[way, s, rows] = mine.astype(bf)
                copy = remote(
                    sent.at[way, s, rows], got.at[way, s, rows], (ring_send, ring_recv), (way, s, half), ways[way]
                )
                copy.start()
                ring[way, s, half] = copy
        if s == 2:
            for copy in w1:
                copy.wait_recv()
            summed = wside[0].astype(f32)
            for peer in range(1, NSIDE):
                summed = summed + wside[peer].astype(f32)
            wsum[...] = summed.astype(bf)
            for d, peer in enumerate(z_peers):
                to = step_round(z, d + 1, NZ)

                @pl.when(to < LUMPS)
                def _():
                    remote(wsum.at[to], wz.at[z], (w2_send, w2_recv), d, peer).start()
        if s == 4:

            @pl.when(z < LUMPS)
            def _():
                for d, peer in enumerate(z_peers):
                    remote(wsum.at[0], wz.at[z], (w2_send, w2_recv), d, peer).wait_recv()
                wz[z] = wsum[z]
                one = wz[0].astype(f32)
                for peer in range(1, NZ):
                    one = one + wz[peer].astype(f32)
                wone[...] = one.astype(bf)
                for d, peer in enumerate(z_peers):
                    remote(wone, wring.at[z], (w3_send, w3_recv), d, peer).start()
                wring[z] = wone[...]
        if s == 7:
            for d, peer in enumerate(z_peers):

                @pl.when(step_round(z, -d - 1, NZ) < LUMPS)
                def _():
                    remote(wone, wring.at[0], (w3_send, w3_recv), d, peer).wait_recv()
            for d in FAR_FIRST:
                w4.append(remote(wring, wall_ref.at[side], (w4_send, w4_recv), d, peers[d]))
                w4[-1].start()
            wall_ref[side] = wring[...]
    for copy in others:
        copy.wait()
    mixed = mixes[0].astype(f32)
    for peer in range(1, nmp):
        mixed = mixed + mixes[peer].astype(f32)
    mixed_ref[...] = mixed.astype(bf)
    for half in range(2):
        for way in range(2):
            ring[way, HOPS[way] - 1, half].wait_recv()
    total = down_ref[...] + back[...].astype(f32) + share[z]
    for way in range(2):
        total = total + got[way, HOPS[way] - 1].astype(f32)
    total_ref[...] = total.astype(bf)
    for copy in w4:
        copy.wait()
    for copy in list(ring.values()) + list(side_copies.values()) + w1:
        copy.wait_send()
    for d, peer in enumerate(z_peers):

        @pl.when(step_round(z, d + 1, NZ) < LUMPS)
        def _():
            remote(wsum.at[0], wz.at[z], (w2_send, w2_recv), d, peer).wait_send()

    @pl.when(z < LUMPS)
    def _():
        for d, peer in enumerate(z_peers):
            remote(wone, wring.at[0], (w3_send, w3_recv), d, peer).wait_send()


def settle(index, q, da, prior, own, keys, seen, proj, cot):
    bf, f32 = jnp.bfloat16, jnp.float32
    features, width = own.shape[1] // 2, own.shape[1]
    nmp = cot.shape[0] // features
    tail = (ROW_CELLS, width)
    block = (ROWS_BLK,) + tail
    slots = (NSIDE, NZ) + tail
    outs = (nmp, features, CELLS_BLK)
    pieces = (NSIDE, LUMPS, ROW_CELLS, 128)
    piece = pieces[1:]
    scratch = [
        (slots, bf),
        (block, bf),
        (block, f32),
        (q.shape, bf),
        (outs, bf),
        (pieces, bf),
        (slots, bf),
        ((NZ,) + block, f32),
        ((2, HOPS[0]) + block, bf),
        ((2, HOPS[0]) + block, bf),
        (block, bf),
        (outs, bf),
        (pieces, bf),
        (piece, bf),
        ((NZ,) + piece[1:], bf),
        (piece[1:], bf),
        (piece, bf),
    ]
    sems = pair_sems(2, HOPS[0], 2) + pair_sems(NZ, NSIDE - 1) + pair_sems(nmp - 1) + pair_sems(1)
    sems += pair_sems(NSIDE - 1) + pair_sems(NZ - 1) + pair_sems(NZ - 1) + pair_sems(NSIDE - 1)
    return pl.pallas_call(
        functools.partial(settle_kernel, nmp),
        in_specs=[pl.BlockSpec(memory_space=pltpu.SMEM)] + [vmem()] * 8,
        out_specs=[vmem()] * 4,
        out_shape=[
            jax.ShapeDtypeStruct(block, bf),
            jax.ShapeDtypeStruct(q.shape, bf),
            jax.ShapeDtypeStruct(q.shape, bf),
            jax.ShapeDtypeStruct(pieces, bf),
        ],
        scratch_shapes=[pltpu.VMEM(*shape) for shape in scratch] + sems,
        compiler_params=pltpu.CompilerParams(collective_id=1, has_side_effects=True),
        name="settle",
    )(index, q, da, prior, own, keys, seen, proj, cot)


def on_device(
    queries, key_cells, value_cells, out_weight, out_cotangent, parent_rows, window_reach, valid_cells
):
    bf, f32 = jnp.bfloat16, jnp.float32
    features = queries.shape[0]
    heads = features // HEAD_DIM
    width = 2 * features
    x_at, z_at, c_at = (lax.axis_index(name) for name in ROW)
    block_id = (x_at * NZ + z_at) * NC + c_at
    valid = valid_cells[0]
    pairs = jnp.concatenate(
        [key_cells.reshape(heads, HEAD_DIM, -1), value_cells.reshape(heads, HEAD_DIM, -1)], axis=1
    )
    own = pairs.reshape(width, CELLS_BLK).T
    nmp = lax.axis_size("mp")
    wanted = parent_rows.reshape(-1)
    lanes = jnp.concatenate([wanted, valid_cells, jnp.zeros(127 - wanted.shape[0], jnp.int32)])
    info = jnp.broadcast_to(lanes, (8, 128))
    slots, index, cotangents, prior, told = fetch(
        own.reshape(ROWS_BLK, ROW_CELLS, width), info, out_cotangent, nmp, wanted.shape[0]
    )
    cotangent_all = cotangents.reshape(-1, CELLS_BLK)
    prior = prior.reshape(CELLS_BLK, width)
    prior_valid = told[0, wanted.shape[0]]
    side_ids = jnp.arange(NSIDE)
    slot_owner = ((side_ids // NC)[:, None] * NZ + jnp.arange(NZ)[None, :]) * NC + (side_ids % NC)[:, None]
    slot_seen = jnp.any(slot_owner.reshape(-1)[:, None] == (wanted // ROWS_BLK)[None, :], axis=-1)
    cell_ids = jnp.arange(CELLS_BLK)
    prior_seen = (cell_ids < prior_valid) & (window_reach[0] == 1) & (block_id > 0)
    seen = jnp.concatenate([prior_seen, cell_ids < valid, jnp.repeat(slot_seen, ROW_CELLS)])
    seen = seen.astype(f32)[:, None]

    d_attended = jnp.dot(out_weight, cotangent_all, preferred_element_type=f32).astype(bf)
    total, mixed, d_queries, weight_all = settle(
        index,
        queries,
        d_attended,
        prior,
        own,
        slots.reshape(SLOTS * ROW_CELLS, width),
        seen,
        out_weight,
        cotangent_all,
    )
    high, wide = features // ROW_CELLS, out_weight.shape[1] // 128
    weight_grad = weight_all.reshape(high, wide, ROW_CELLS, 128).transpose(0, 2, 1, 3)
    weight_grad = weight_grad.reshape(features, -1).astype(f32)
    d_pairs = total.reshape(CELLS_BLK, width).T.reshape(heads, 2, HEAD_DIM, CELLS_BLK)
    d_key_cells = d_pairs[:, 0].reshape(features, CELLS_BLK)
    d_value_cells = d_pairs[:, 1].reshape(features, CELLS_BLK)
    return mixed, d_queries, d_key_cells, d_value_cells, weight_grad


def solution(mesh):
    fine = Mesh(mesh.devices.reshape(NX, NZ, NC, -1), ROW + ("mp",))
    split = P("mp", ROW)
    return jax.shard_map(
        on_device,
        mesh=fine,
        in_specs=(split, split, split, P("mp", None), split, P(ROW, None), P(ROW), P(ROW)),
        out_specs=(split, split, split, split, P("mp", None)),
        check_vma=False,
    )
```
